32 devices in a mesh: groups: 2 (over x), seq: 16 (over z, y, core).
Axes of the slice: x: 2, y: 2, z: 4, core: 2. Of those that a mesh axis runs over, the one named last changes fastest.
Arguments:
- residual: float32 [4, 16, 128, 1152], P('groups', 'seq'), parts along dimension 0, may hold values from -16 to 16
- w_qkv: bfloat16 [1152, 3456], replicated, may hold values from -0.15 to 0.15
- w_proj: bfloat16 [1152, 1152], replicated, may hold values from -0.1875 to 0.1875
- q_gain: float32 [1152], replicated, may hold values from 0.5 to 7
- k_gain: float32 [1152], replicated, may hold values from 0.5 to 7
- step_mods: float32 [30, 3, 1152], replicated, may hold values from -4 to 4
- timestep: int32 [2], P('groups'), parts along dimension 0, may hold values from 0 to 29, as said below
Outputs:
- updated: float32 [4, 16, 128, 1152], P('groups', 'seq'), parts along dimension 0
The draws below stay inside these ranges and needn't reach their ends.
There are 2 independent parts, one for each index of `groups`. The reference program is written for one: setup_inputs(seed, part) draws one part's arguments, and reference() takes and returns one part's arrays. A program takes and returns all parts, laid end to end along the dimension named above; an argument that names none is the same for every part. Nothing has to cross between parts.
Inputs may be any that keep to these rules, and one draw needn't show every extreme that they name: `timestep`: the first part takes a step from the first half of the table, the second part the last step.
All inputs are finite; a program needn't handle non-finite values.
Results may differ from the reference program's by a relative error of at most 0.002.
Values may be sent and summed in bfloat16 or wider, within the bound.
No kernel may reach another device: no remote copies, remote signals or barrier semaphores. Data moves between devices by JAX's collectives and lax.ppermute only.
A program may use at most 64 MiB of HBM per device.

```python
import jax
import jax.numpy as jnp
from jax import lax

D = 1152
HEADS = 16
HEAD_DIM = 72
STEPS = 30
PATCHES = 128
FRAMES = 16


def gain_draw(key, member):
    single = jax.random.uniform(jax.random.fold_in(key, 11 + member), (HEADS, HEAD_DIM), jnp.float32, 0.0, 1.0)
    gains = jnp.exp(jnp.log(0.8) + single * (jnp.log(2.0) - jnp.log(0.8)))
    return gains.reshape(D)


def draw_q_gain(key, part):
    return gain_draw(key, 0)


def draw_k_gain(key, part):
    return gain_draw(key, 1)


def draw_timestep(key, part):
    half = STEPS // 2
    start = jax.random.randint(jax.random.fold_in(key, 31), (1,), 0, half, jnp.int32)
    side = jnp.asarray(part, jnp.int32) % 2
    last_step = jnp.full((1,), STEPS - 1, jnp.int32)
    return jnp.where(side == 1, last_step, start).astype(jnp.int32)


def draw_w_qkv(key, part):
    spread = D ** (-0.5)
    inner_key = jax.random.fold_in(key, 1)
    base_draw = jax.random.normal(inner_key, (D, 3 * D), jnp.float32) * spread
    return jnp.clip(base_draw, -0.149, 0.149).astype(jnp.bfloat16)


def draw_residual(key, part):
    column_scale = jnp.exp(jax.random.uniform(jax.random.fold_in(key, 2), (D,), jnp.float32, -1.1513, 1.1513))
    offset = 0.5 * jax.random.normal(jax.random.fold_in(key, 3), (D,), jnp.float32)
    row_scale = jnp.exp(jax.random.uniform(jax.random.fold_in(key, 6), (2, FRAMES, PATCHES, 1), jnp.float32, -1.1513, 1.1513))
    values = jax.random.normal(jax.random.fold_in(key, 4), (2, FRAMES, PATCHES, D), jnp.float32) * row_scale * column_scale + offset
    return jnp.clip(values, -16.0, 16.0)


def bell_draw(key, extent, scale, reach, held_as=jnp.bfloat16):
    values = jax.random.normal(key, extent, jnp.float32) * scale
    return jnp.minimum(jnp.maximum(values, -reach), reach).astype(held_as)


def setup_inputs(seed: int = 0, part: int = 0) -> dict:
    keys = jax.random.split(jax.random.key(seed), 8)
    own_keys = jax.random.split(jax.random.fold_in(keys[7], part), 8)
    return {
        "residual": draw_residual(jax.random.fold_in(jax.random.fold_in(keys[7], part), 71), part),
        "w_qkv": draw_w_qkv(jax.random.fold_in(keys[7], 71), part),
        "w_proj": bell_draw(keys[2], (D, D), D ** -0.5, 0.1875),
        "q_gain": draw_q_gain(jax.random.fold_in(keys[7], 71), part),
        "k_gain": draw_k_gain(jax.random.fold_in(keys[7], 71), part),
        "step_mods": bell_draw(keys[5], (STEPS, 3, D), 0.8, 4.0, jnp.float32),
        "timestep": draw_timestep(jax.random.fold_in(jax.random.fold_in(keys[7], part), 71), part),
    }


def layer_modulate(rows, shift_row, scale_row):
    centre = lax.optimization_barrier(jnp.mean(rows, axis=-1, keepdims=True))
    centred = rows - centre
    variance = lax.optimization_barrier(jnp.mean(centred * centred, axis=-1, keepdims=True))
    return (centred * lax.rsqrt(variance + 1e-06) * (1.0 + scale_row) + shift_row).astype(jnp.bfloat16)

def head_norm(vectors, gain):
    square = lax.optimization_barrier(jnp.mean(vectors * vectors, axis=-1, keepdims=True))
    return (vectors * lax.rsqrt(square + 1e-06) * gain).astype(jnp.bfloat16)

def one_patch(items):
    queries, key_vecs, values = items
    queries = lax.optimization_barrier(queries).astype(jnp.float32)
    key_vecs = lax.optimization_barrier(key_vecs).astype(jnp.float32)
    values = lax.optimization_barrier(values).astype(jnp.float32)
    scores = jnp.einsum('bqhd,bkhd->bhqk', queries, key_vecs, precision=lax.Precision.HIGHEST) * HEAD_DIM ** (-0.5)
    top = lax.optimization_barrier(jnp.max(scores, axis=-1, keepdims=True))
    weights = jnp.exp(scores - top)
    total = lax.optimization_barrier(jnp.sum(weights, axis=-1, keepdims=True))
    probs = (weights / total).astype(jnp.bfloat16)
    probs = lax.optimization_barrier(probs).astype(jnp.float32)
    mixed = jnp.einsum('bhqk,bkhd->bqhd', probs, values, precision=lax.Precision.HIGHEST)
    return mixed.astype(jnp.bfloat16)

def reference(residual, w_qkv, w_proj, q_gain, k_gain, step_mods, timestep):
    modulation = lax.dynamic_index_in_dim(step_mods, timestep[0], 0, keepdims=False)
    shift_row = modulation[0]
    scale_row = modulation[1]
    gate_row = modulation[2]
    branch, frames, patches, width = residual.shape
    modulated = layer_modulate(residual, shift_row, scale_row)
    projected = jnp.dot(modulated.reshape(-1, width), w_qkv, preferred_element_type=jnp.float32)
    projected = projected.reshape(branch, frames, patches, 3, HEADS, HEAD_DIM)
    queries = head_norm(projected[:, :, :, 0], q_gain.reshape(HEADS, HEAD_DIM))
    key_vecs = head_norm(projected[:, :, :, 1], k_gain.reshape(HEADS, HEAD_DIM))
    values = projected[:, :, :, 2].astype(jnp.bfloat16)
    stacked = (jnp.moveaxis(queries, 2, 0), jnp.moveaxis(key_vecs, 2, 0), jnp.moveaxis(values, 2, 0))
    attended = jnp.moveaxis(lax.map(one_patch, stacked), 0, 2).reshape(branch, frames, patches, width)
    output = jnp.dot(attended.reshape(-1, width), w_proj, preferred_element_type=jnp.float32)
    return residual + gate_row * output.reshape(residual.shape)
```

```python
import functools

import jax
import jax.numpy as jnp
from jax import lax
from jax.experimental import pallas as pl
from jax.experimental.pallas import tpu as pltpu
from jax.sharding import PartitionSpec as P

HEADS = 16
HEAD_DIM = 72
LANES = 128
F32 = jnp.float32
BF16 = jnp.bfloat16
VMEM = pltpu.VMEM


def modulate_kernel(step_ref, rows_ref, mods_ref, out_ref):
    del step_ref
    rows = rows_ref[0]
    shift_row, scale_row = mods_ref[0, 0:1, :], mods_ref[0, 1:2, :]
    centre = jnp.mean(rows, axis=-1, keepdims=True)
    centred = rows - centre
    variance = jnp.mean(centred * centred, axis=-1, keepdims=True)
    normed = centred * lax.rsqrt(variance + 1e-06) * (1.0 + scale_row) + shift_row
    out_ref[:, 0] = normed.reshape(out_ref.shape[0], *out_ref.shape[2:]).astype(BF16)


def modulate(rows, step_mods, timestep, n):
    branch, patches, width = rows.shape
    share = patches // n
    return pl.pallas_call(
        modulate_kernel,
        out_shape=jax.ShapeDtypeStruct((n, branch, share, width), BF16),
        grid_spec=pltpu.PrefetchScalarGridSpec(
            num_scalar_prefetch=1,
            grid=(branch,),
            in_specs=[
                pl.BlockSpec((1, patches, width), lambda b, step: (b, 0, 0)),
                pl.BlockSpec((1, 3, width), lambda b, step: (step[0], 0, 0)),
            ],
            out_specs=pl.BlockSpec((n, 1, share, width), lambda b, step: (0, b, 0, 0)),
        ),
        name="modulate",
    )(timestep, rows, step_mods)


def split_dot(wide, ones):
    high = wide.astype(BF16)
    low = (wide - high.astype(F32)).astype(BF16)
    return jnp.dot(high, ones, preferred_element_type=F32) + jnp.dot(
        low, ones, preferred_element_type=F32
    )


def head_of(shape, feature_dim, head_dim):
    feature = lax.broadcasted_iota(jnp.int32, shape, feature_dim)
    first = lax.broadcasted_iota(jnp.int32, shape, head_dim) * HEAD_DIM
    inside = (feature >= first) & (feature < first + HEAD_DIM)
    return jnp.where(inside, 1.0, 0.0).astype(BF16)


def attend_kernel(x_ref, w_ref, q_gain_ref, k_gain_ref, out_ref, q_ref, k_ref, v_ref):
    frames, branch, share, width = x_ref.shape
    tokens = frames * share
    x = x_ref[...].reshape(frames * branch * share, width)
    gather = head_of((width, LANES), 0, 1)
    spread = head_of((LANES, width), 1, 0)

    def per_branch(values, ref):
        values = values.reshape(frames, branch, share, width)
        for b in range(branch):
            ref[b] = values[:, b].reshape(tokens, width).astype(BF16)

    for part, gain_ref, ref in ((0, q_gain_ref, q_ref), (1, k_gain_ref, k_ref)):
        vectors = jnp.dot(
            x, w_ref[:, part * width : (part + 1) * width], preferred_element_type=F32
        )
        square = split_dot(vectors * vectors, gather) * (1.0 / HEAD_DIM)
        factor = split_dot(lax.rsqrt(square + 1e-06), spread)
        per_branch(vectors * factor * gain_ref[...], ref)
    per_branch(jnp.dot(x, w_ref[:, 2 * width :], preferred_element_type=F32), v_ref)

    same = lax.broadcasted_iota(jnp.int32, (share, tokens), 0) == lax.rem(
        lax.broadcasted_iota(jnp.int32, (share, tokens), 1), share
    )
    lane = lax.broadcasted_iota(jnp.int32, (1, 2 * LANES), 1)
    for b in range(branch):
        blocks = {}
        for h in range(HEADS):
            start = h * HEAD_DIM
            low = start // LANES * LANES
            high = min(-(-(start + HEAD_DIM) // LANES) * LANES, width)
            inside = (lane >= start - low) & (lane < start - low + HEAD_DIM)
            inside = inside[:, : high - low]
            query = jnp.where(inside, q_ref[b, :, low:high], jnp.zeros((), BF16))
            scores = lax.dot_general(
                k_ref[b, :, low:high], query, (((1,), (1,)), ((), ())), preferred_element_type=F32
            )
            scores = scores.reshape(frames, share, tokens)
            top = jnp.max(scores, axis=0)
            weights = jnp.exp((scores - top) * HEAD_DIM ** (-0.5))
            total = jnp.sum(weights, axis=0)
            probs = weights * jnp.where(same, 1.0 / total, 0.0)
            probs = probs.reshape(tokens, tokens).astype(BF16)
            mixed = lax.dot_general(
                probs, v_ref[b, :, low:high], (((0,), (0,)), ((), ())), preferred_element_type=F32
            )
            for at in range(low, high, LANES):
                piece = mixed[:, at - low : at - low + LANES]
                if at in blocks:
                    piece = jnp.where(inside[:, at - low : at - low + LANES], piece, blocks[at])
                blocks[at] = piece
            done = [at for at in blocks if at + LANES <= start + HEAD_DIM]
            for at in done:
                block = blocks.pop(at).astype(BF16)
                out_ref[:, b, :, at : at + LANES] = block.reshape(frames, share, LANES)


def attend(x, w_qkv, q_gain, k_gain):
    frames, branch, share, width = x.shape
    tokens = frames * share
    return pl.pallas_call(
        attend_kernel,
        out_shape=jax.ShapeDtypeStruct(x.shape, BF16),
        in_specs=[pl.BlockSpec(memory_space=VMEM)] * 4,
        out_specs=pl.BlockSpec(memory_space=VMEM),
        scratch_shapes=[VMEM((branch, tokens, width), BF16)] * 3,
        name="attend",
    )(x, w_qkv, q_gain.reshape(1, width), k_gain.reshape(1, width))


def project_kernel(step_ref, x_ref, w_ref, mods_ref, residual_ref, out_ref):
    del step_ref
    n, branch, share, width = x_ref.shape
    output = jnp.dot(
        x_ref[...].reshape(n * branch * share, width), w_ref[...], preferred_element_type=F32
    )
    gated = mods_ref[0, 2:3, :] * output
    gated = gated.reshape(n, branch, share, -1)
    for b in range(branch):
        out_ref[b] = residual_ref[b] + gated[:, b].reshape(n * share, -1)


def project(x, w_proj, step_mods, timestep, rows):
    n, branch, share, width = x.shape
    cols = 384
    return pl.pallas_call(
        project_kernel,
        out_shape=jax.ShapeDtypeStruct(rows.shape, F32),
        grid_spec=pltpu.PrefetchScalarGridSpec(
            num_scalar_prefetch=1,
            grid=(width // cols,),
            in_specs=[
                pl.BlockSpec((n, branch, share, width), lambda j, step: (0, 0, 0, 0)),
                pl.BlockSpec((width, cols), lambda j, step: (0, j)),
                pl.BlockSpec((1, 3, cols), lambda j, step: (step[0], 0, j)),
                pl.BlockSpec((branch, n * share, cols), lambda j, step: (0, 0, j)),
            ],
            out_specs=pl.BlockSpec((branch, n * share, cols), lambda j, step: (0, 0, j)),
        ),
        name="project",
    )(timestep, x, w_proj, step_mods, rows)


def body(n, residual, w_qkv, w_proj, q_gain, k_gain, step_mods, timestep):
    rows = residual[:, 0]
    swap = functools.partial(
        lax.all_to_all, axis_name="seq", split_axis=0, concat_axis=0, tiled=True
    )
    modulated = swap(modulate(rows, step_mods, timestep, n))
    attended = swap(attend(modulated, w_qkv, q_gain, k_gain))
    return project(attended, w_proj, step_mods, timestep, rows)[:, None]


def solution(mesh):
    in_specs = (P("groups", "seq", None, None), P(), P(), P(), P(), P(), P("groups"))
    out_specs = P("groups", "seq", None, None)
    step = functools.partial(body, mesh.shape["seq"])
    return jax.shard_map(step, mesh=mesh, in_specs=in_specs, out_specs=out_specs, check_vma=False)
```

```python
import functools

import jax
import jax.numpy as jnp
from jax import lax
from jax.experimental import pallas as pl
from jax.experimental.pallas import tpu as pltpu
from jax.sharding import PartitionSpec as P

HEADS = 16
HEAD_DIM = 72
LANES = 128
LOG2_E = 1.4426950408889634
F32 = jnp.float32
BF16 = jnp.bfloat16
VMEM = pltpu.VMEM


def params(mebibytes):
    return pltpu.CompilerParams(vmem_limit_bytes=mebibytes << 20)


def in_hbm(array):
    return pltpu.with_memory_space_constraint(array, pltpu.HBM)


def block_of(j, r, exchange):
    if not exchange:
        return j
    me = lax.axis_index("seq")
    return jnp.bitwise_xor(me, 2 * j + r)


def modulate_kernel(exchange, step_ref, rows_hbm, mods_hbm, *refs):
    *out_refs, gate_ref, rows_ref, mods_ref, sems = refs
    branch, patches, width = rows_ref.shape
    count, _, share, _ = out_refs[0].shape

    def fetch(b):
        return pltpu.make_async_copy(rows_hbm.at[b], rows_ref.at[b], sems.at[b])

    mods = pltpu.make_async_copy(mods_hbm, mods_ref, sems.at[branch])
    fetch(0).start()
    mods.start()
    for b in range(1, branch):
        fetch(b).start()
    mods.wait()
    step = pl.ds(step_ref[0], 1)
    shift_row, scale_row = mods_ref[0, step, :], 1.0 + mods_ref[1, step, :]
    gate_ref[...] = mods_ref[2, step, :]
    group = 1 if exchange else max(1, 32 // share)
    for b in range(branch):
        fetch(b).wait()
        for r, out_ref in enumerate(out_refs):
            for j in range(0, count, group):
                start = block_of(j, r, exchange) * share
                if exchange:
                    start = pl.multiple_of(start, share)
                rows = rows_ref[b, pl.ds(start, group * share)]
                centre = jnp.mean(rows, axis=-1, keepdims=True)
                centred = rows - centre
                variance = jnp.mean(centred * centred, axis=-1, keepdims=True)
                normed = centred * lax.rsqrt(variance + 1e-06) * scale_row + shift_row
                out_ref[j : j + group, b] = normed.reshape(group, share, width).astype(BF16)


def modulate(rows, step_mods, timestep, n, exchange):
    branch, patches, width = rows.shape
    outs = 2 if exchange else 1
    part = VMEM((n // outs, branch, patches // n, width), BF16)
    return pl.pallas_call(
        functools.partial(modulate_kernel, exchange),
        out_shape=[part] * outs + [VMEM((1, width), F32)],
        in_specs=[
            pl.BlockSpec(memory_space=pltpu.SMEM),
            pl.BlockSpec(memory_space=pltpu.HBM),
            pl.BlockSpec(memory_space=pltpu.HBM),
        ],
        out_specs=[pl.BlockSpec(memory_space=VMEM)] * (outs + 1),
        scratch_shapes=[
            VMEM((branch, patches, width), F32),
            VMEM((3, step_mods.shape[0], width), F32),
            pltpu.SemaphoreType.DMA((branch + 1,)),
        ],
        compiler_params=params(8),
        name="modulate",
    )(timestep, in_hbm(rows), in_hbm(jnp.swapaxes(step_mods, 0, 1)))


def stage_kernel(after_ref, w_hbm, w_ref, sem):
    del after_ref
    copy = pltpu.make_async_copy(w_hbm, w_ref, sem)
    copy.start()
    copy.wait()


def stage(w, after):
    return pl.pallas_call(
        stage_kernel,
        out_shape=VMEM(w.shape, w.dtype),
        in_specs=[pl.BlockSpec(memory_space=VMEM), pl.BlockSpec(memory_space=pltpu.HBM)],
        out_specs=pl.BlockSpec(memory_space=VMEM),
        scratch_shapes=[pltpu.SemaphoreType.DMA],
        compiler_params=params(1),
        name="stage",
    )(after, in_hbm(w))


def pack_kernel(keep_ref, got_ref, *out_refs):
    for j, out_ref in enumerate(out_refs):
        out_ref[0] = keep_ref[j]
        out_ref[1] = got_ref[j]


def pack(keep, got):
    count, *part = keep.shape
    return pl.pallas_call(
        pack_kernel,
        out_shape=[VMEM((2, *part), keep.dtype)] * count,
        in_specs=[pl.BlockSpec(memory_space=VMEM)] * 2,
        out_specs=[pl.BlockSpec(memory_space=VMEM)] * count,
        compiler_params=params(1),
        name="pack",
    )(keep, got)


def swap_parts(n, keep, give):
    got = lax.ppermute(give, "seq", [(s, s ^ 1) for s in range(n)])
    parts = pack(keep, got)
    return [parts[0]] + [
        lax.ppermute(parts[j], "seq", [(s, s ^ (2 * j)) for s in range(n)])
        for j in range(1, n // 2)
    ]


def gather_rows(x_refs):
    return jnp.concatenate([ref[...].reshape(-1, ref.shape[-1]) for ref in x_refs], axis=0)


def head_of(shape, feature_dim):
    feature = lax.broadcasted_iota(jnp.int32, shape, feature_dim)
    place = lax.broadcasted_iota(jnp.int32, shape, 1 - feature_dim)
    first = lax.rem(place, HEADS) * HEAD_DIM
    inside = (feature >= first) & (feature < first + HEAD_DIM) & (place < 2 * HEADS)
    return jnp.where(inside, 1.0, 0.0).astype(BF16)


def high_low(wide):
    high = wide.astype(BF16)
    return high, wide - high.astype(F32)


def head_scale(vectors, gather, spread):
    high, low = high_low(vectors * vectors)
    square = jnp.dot(high, gather, preferred_element_type=F32)
    square += jnp.dot(low.astype(BF16), gather, preferred_element_type=F32)
    high, low = high_low(lax.rsqrt(square * (1.0 / HEAD_DIM) + 1e-06))
    place = lax.broadcasted_iota(jnp.int32, low.shape, 1)
    both = jnp.where(place < HEADS, high.astype(F32), low).astype(BF16)
    return vectors * jnp.dot(both, spread, preferred_element_type=F32)


def attend_kernel(ins, outs, *refs):
    x_refs, (w_ref, q_gain_ref, k_gain_ref) = refs[:ins], refs[ins : ins + 3]
    out_refs, (q_ref, k_ref, v_ref) = refs[ins + 3 : ins + 3 + outs], refs[ins + 3 + outs :]
    _, branch, share, width = x_refs[0].shape
    x = gather_rows(x_refs)
    tokens = x.shape[0] // branch
    frames = tokens // share
    gather = head_of((width, LANES), 0)
    spread = head_of((LANES, width), 1)
    window = 2 * LANES
    lane = lax.broadcasted_iota(jnp.int32, (1, window), 1)
    pairs = []
    for i in range(HEADS // 2):
        masks = []
        for h in (2 * i, 2 * i + 1):
            start = h * HEAD_DIM - i * LANES
            masks.append(jnp.where((lane >= start) & (lane < start + HEAD_DIM), 1.0, 0.0))
        pairs.append((i * LANES, masks))

    def product(part):
        values = jnp.dot(
            x, w_ref[:, part * width : (part + 1) * width], preferred_element_type=F32
        )
        return values

    def per_branch(values):
        values = values.reshape(frames, branch, share, width)
        return [values[:, b].reshape(tokens, width) for b in range(branch)]

    def store_pairs(values, rows, ref):
        for b, own in enumerate(per_branch(values)):
            for i, (at, masks) in enumerate(pairs):
                for side, mask in enumerate(masks):
                    row = mask if rows is None else mask * rows[:, at : at + window]
                    ref[b, i, side * tokens : (side + 1) * tokens] = (
                        own[:, at : at + window] * row
                    ).astype(BF16)

    store_pairs(head_scale(product(0), gather, spread), q_gain_ref[...], q_ref)
    for b, own in enumerate(per_branch(head_scale(product(1), gather, spread))):
        k_ref[b] = (own * k_gain_ref[...]).astype(BF16)
    store_pairs(product(2), None, v_ref)

    same = lax.broadcasted_iota(jnp.int32, (share, 2 * tokens), 0) == lax.rem(
        lax.broadcasted_iota(jnp.int32, (share, 2 * tokens), 1), share
    )

    def emit(b, at, block):
        block = block.astype(BF16).reshape(frames // outs, outs, share, LANES)
        for r, out_ref in enumerate(out_refs):
            out_ref[:, b, :, at : at + LANES] = block[:, r]

    carry = [None] * branch
    for i, (at, _) in enumerate(pairs):
        for b in range(branch):
            scores = lax.dot_general(
                k_ref[b, :, at : at + window],
                q_ref[b, i],
                (((1,), (1,)), ((), ())),
                preferred_element_type=F32,
            ).reshape(frames, share, 2 * tokens)
            top = jnp.max(scores, axis=0)
            weights = jnp.exp2((scores - top) * (HEAD_DIM ** (-0.5) * LOG2_E))
            total = jnp.sum(weights, axis=0)
            probs = weights * jnp.where(same, 1.0 / total, 0.0)
            probs = probs.reshape(tokens, 2 * tokens).astype(BF16)
            probs = jnp.concatenate([probs[:, :tokens], probs[:, tokens:]], axis=0)
            mixed = lax.dot_general(
                probs, v_ref[b, i], (((0,), (0,)), ((), ())), preferred_element_type=F32
            )
            block = mixed[:, :LANES]
            if carry[b] is not None:
                block = block + carry[b]
            carry[b] = mixed[:, LANES:]
            emit(b, at, block)
    for b in range(branch):
        emit(b, width - LANES, carry[b])


def attend(xs, w_qkv, q_gain, k_gain, outs):
    frames = sum(x.shape[0] for x in xs)
    _, branch, share, width = xs[0].shape
    tokens = frames * share
    pair_shape = (branch, HEADS // 2, 2 * tokens, 2 * LANES)
    return pl.pallas_call(
        functools.partial(attend_kernel, len(xs), outs),
        out_shape=[VMEM((frames // outs, branch, share, width), BF16)] * outs,
        in_specs=[pl.BlockSpec(memory_space=VMEM)] * (len(xs) + 3),
        out_specs=[pl.BlockSpec(memory_space=VMEM)] * outs,
        scratch_shapes=[
            VMEM(pair_shape, BF16),
            VMEM((branch, tokens, width), BF16),
            VMEM(pair_shape, BF16),
        ],
        compiler_params=params(24),
        name="attend",
    )(*xs, w_qkv, q_gain.reshape(1, width), k_gain.reshape(1, width))


def project_kernel(exchange, ins, *refs):
    x_refs, (w_ref, gate_ref, residual_ref, out_ref) = refs[:ins], refs[ins:]
    _, branch, share, width = x_refs[0].shape
    output = jnp.dot(gather_rows(x_refs), w_ref[...], preferred_element_type=F32)
    gated = (gate_ref[...] * output).reshape(-1, branch, share, output.shape[-1])
    for b in range(branch):
        if not exchange:
            out_ref[b] = residual_ref[b] + gated[:, b].reshape(out_ref.shape[1:])
            continue
        for at in range(gated.shape[0]):
            start = pl.multiple_of(block_of(at // 2, at % 2, exchange) * share, share)
            block = pl.ds(start, share)
            out_ref[b, block] = residual_ref[b, block] + gated[at, b]


def project(xs, w_proj, gate_row, rows, exchange):
    branch, patches, width = rows.shape
    cols = 384
    return pl.pallas_call(
        functools.partial(project_kernel, exchange, len(xs)),
        out_shape=jax.ShapeDtypeStruct(rows.shape, F32),
        grid=(width // cols,),
        in_specs=[pl.BlockSpec(x.shape, lambda j: (0, 0, 0, 0)) for x in xs]
        + [
            pl.BlockSpec((width, cols), lambda j: (0, j)),
            pl.BlockSpec((1, cols), lambda j: (0, j)),
            pl.BlockSpec((branch, patches, cols), lambda j: (0, 0, j)),
        ],
        out_specs=pl.BlockSpec((branch, patches, cols), lambda j: (0, 0, j)),
        compiler_params=params(12),
        name="project",
    )(*xs, w_proj, gate_row, rows)


def body(n, residual, w_qkv, w_proj, q_gain, k_gain, step_mods, timestep):
    rows = residual[:, 0]
    share = rows.shape[1] // n
    exchange = 2 <= n <= 32 and n & (n - 1) == 0 and share % 8 == 0
    if exchange:
        swap = functools.partial(swap_parts, n)
    else:

        def swap(parts):
            return [lax.all_to_all(parts, "seq", split_axis=0, concat_axis=0, tiled=True)]

    *parts, gate_row = modulate(rows, step_mods, timestep, n, exchange)
    w_qkv = stage(w_qkv, gate_row)
    parts = attend(swap(*parts), w_qkv, q_gain, k_gain, len(parts))
    return project(swap(*parts), w_proj, gate_row, rows, exchange)[:, None]


def solution(mesh):
    in_specs = (P("groups", "seq", None, None), P(), P(), P(), P(), P(), P("groups"))
    out_specs = P("groups", "seq", None, None)
    step = functools.partial(body, mesh.shape["seq"])
    return jax.shard_map(step, mesh=mesh, in_specs=in_specs, out_specs=out_specs, check_vma=False)
```

```python
import functools

import jax
import jax.numpy as jnp
from jax import lax
from jax.experimental import pallas as pl
from jax.experimental.pallas import tpu as pltpu
from jax.sharding import PartitionSpec as P

HEADS = 16
HEAD_DIM = 72
LANES = 128
LOG2_E = 1.4426950408889634
F32 = jnp.float32
BF16 = jnp.bfloat16
VMEM = pltpu.VMEM


def params(mebibytes):
    return pltpu.CompilerParams(vmem_limit_bytes=mebibytes << 20)


def in_hbm(array):
    return pltpu.with_memory_space_constraint(array, pltpu.HBM)


def block_of(j, r, exchange):
    if not exchange:
        return j
    me = lax.axis_index("seq")
    return jnp.bitwise_xor(me, 2 * j + r)


def modulate_kernel(exchange, step_ref, rows_hbm, mods_hbm, *refs):
    *out_refs, gate_ref, rows_ref, mods_ref, sems = refs
    branch, _, width = rows_ref.shape
    count, _, share, _ = out_refs[0].shape

    def fetch(b):
        return pltpu.make_async_copy(rows_hbm.at[b], rows_ref.at[b], sems.at[b])

    mods = pltpu.make_async_copy(mods_hbm, mods_ref, sems.at[branch])
    fetch(0).start()
    mods.start()
    for b in range(1, branch):
        fetch(b).start()
    mods.wait()
    step = pl.ds(step_ref[0], 1)
    shift_row, scale_row = mods_ref[0, step, :], 1.0 + mods_ref[1, step, :]
    gate_ref[...] = mods_ref[2, step, :]
    group = 1 if exchange else max(1, 32 // share)
    for b in range(branch):
        fetch(b).wait()
        for r, out_ref in enumerate(out_refs):
            for j in range(0, count, group):
                start = block_of(j, r, exchange) * share
                if exchange:
                    start = pl.multiple_of(start, share)
                rows = rows_ref[b, pl.ds(start, group * share)]
                centre = jnp.mean(rows, axis=-1, keepdims=True)
                centred = rows - centre
                variance = jnp.mean(centred * centred, axis=-1, keepdims=True)
                normed = centred * lax.rsqrt(variance + 1e-06) * scale_row + shift_row
                out_ref[j : j + group, b] = normed.reshape(group, share, width).astype(BF16)


def modulate(rows, step_mods, timestep, n, exchange):
    branch, patches, width = rows.shape
    outs = 2 if exchange else 1
    part = VMEM((n // outs, branch, patches // n, width), BF16)
    return pl.pallas_call(
        functools.partial(modulate_kernel, exchange),
        out_shape=[part] * outs + [VMEM((1, width), F32)],
        in_specs=[
            pl.BlockSpec(memory_space=pltpu.SMEM),
            pl.BlockSpec(memory_space=pltpu.HBM),
            pl.BlockSpec(memory_space=pltpu.HBM),
        ],
        out_specs=[pl.BlockSpec(memory_space=VMEM)] * (outs + 1),
        scratch_shapes=[
            VMEM((branch, patches, width), F32),
            VMEM((3, step_mods.shape[0], width), F32),
            pltpu.SemaphoreType.DMA((branch + 1,)),
        ],
        compiler_params=params(8),
        name="modulate",
    )(timestep, in_hbm(rows), in_hbm(jnp.swapaxes(step_mods, 0, 1)))


def fetch_columns(w_hbm, part, w_ref, sem):
    return pltpu.make_async_copy(
        w_hbm.at[:, pl.ds(part * w_ref.shape[1], w_ref.shape[1])], w_ref, sem
    )


def stage_first_kernel(after_ref, w_hbm, w_ref, sem):
    del after_ref
    copy = fetch_columns(w_hbm, 0, w_ref, sem)
    copy.start()
    copy.wait()


def stage_first(w, after):
    width = w.shape[0]
    return pl.pallas_call(
        stage_first_kernel,
        out_shape=VMEM((width, width), w.dtype),
        in_specs=[pl.BlockSpec(memory_space=VMEM), pl.BlockSpec(memory_space=pltpu.HBM)],
        out_specs=pl.BlockSpec(memory_space=VMEM),
        scratch_shapes=[pltpu.SemaphoreType.DMA],
        compiler_params=params(1),
        name="stage_first",
    )(after, in_hbm(w))


def stage_rest_kernel(after_ref, w_hbm, q_gain_hbm, k_gain_hbm, *refs):
    wk_ref, wv_ref, gather_ref, spread_ref, q_row_ref, k_row_ref, line_ref, sems = refs
    del after_ref
    gains = [
        pltpu.make_async_copy(gain, line_ref.at[at], sems.at[at])
        for at, gain in enumerate((q_gain_hbm, k_gain_hbm))
    ]
    columns = [
        fetch_columns(w_hbm, part, ref, sems.at[part + 1])
        for part, ref in ((1, wk_ref), (2, wv_ref))
    ]
    for copy in gains + columns:
        copy.start()
    gather_ref[...] = head_of(gather_ref.shape, 0)
    spread_ref[...] = head_of(spread_ref.shape, 1)
    for at, row_ref in enumerate((q_row_ref, k_row_ref)):
        gains[at].wait()
        row_ref[...] = line_ref[at].reshape(row_ref.shape)
    for copy in columns:
        copy.wait()


def stage_rest(w, q_gain, k_gain, after):
    width = w.shape[0]
    hbm = pl.BlockSpec(memory_space=pltpu.HBM)
    return pl.pallas_call(
        stage_rest_kernel,
        out_shape=[
            VMEM((width, width), w.dtype),
            VMEM((width, width), w.dtype),
            VMEM((width, LANES), BF16),
            VMEM((LANES, width), BF16),
            VMEM((1, width), F32),
            VMEM((1, width), F32),
        ],
        in_specs=[pl.BlockSpec(memory_space=VMEM), hbm, hbm, hbm],
        out_specs=[pl.BlockSpec(memory_space=VMEM)] * 6,
        scratch_shapes=[VMEM((2, width), F32), pltpu.SemaphoreType.DMA((4,))],
        compiler_params=params(2),
        name="stage_rest",
    )(after, in_hbm(w), in_hbm(q_gain), in_hbm(k_gain))


def pack_kernel(keep_ref, got_ref, *out_refs):
    for j, out_ref in enumerate(out_refs):
        out_ref[0] = keep_ref[j]
        out_ref[1] = got_ref[j]


def pack(keep, got):
    count, *part = keep.shape
    return pl.pallas_call(
        pack_kernel,
        out_shape=[VMEM((2, *part), keep.dtype)] * count,
        in_specs=[pl.BlockSpec(memory_space=VMEM)] * 2,
        out_specs=[pl.BlockSpec(memory_space=VMEM)] * count,
        compiler_params=params(1),
        name="pack",
    )(keep, got)


def send_order(n):
    return [*range(n // 4, n // 2), *range(1, n // 4)]


def swap_parts(n, keep, give):
    got = lax.ppermute(give, "seq", [(s, s ^ 1) for s in range(n)])
    parts = list(pack(keep, got))
    for j in send_order(n):
        parts[j] = lax.ppermute(parts[j], "seq", [(s, s ^ (2 * j)) for s in range(n)])
    return parts


def gather_rows(x_refs):
    return jnp.concatenate([ref[...].reshape(-1, ref.shape[-1]) for ref in x_refs], axis=0)


def head_of(shape, feature_dim):
    feature = lax.broadcasted_iota(jnp.int32, shape, feature_dim)
    place = lax.broadcasted_iota(jnp.int32, shape, 1 - feature_dim)
    first = lax.rem(place, HEADS) * HEAD_DIM
    inside = (feature >= first) & (feature < first + HEAD_DIM) & (place < 2 * HEADS)
    return jnp.where(inside, 1.0, 0.0).astype(BF16)


def high_low(wide):
    high = wide.astype(BF16)
    return high, wide - high.astype(F32)


def head_scale(vectors, gather, spread):
    high, low = high_low(vectors * vectors)
    square = jnp.dot(high, gather, preferred_element_type=F32)
    square += jnp.dot(low.astype(BF16), gather, preferred_element_type=F32)
    high, low = high_low(lax.rsqrt(square * (1.0 / HEAD_DIM) + 1e-06))
    place = lax.broadcasted_iota(jnp.int32, low.shape, 1)
    both = jnp.where(place < HEADS, high.astype(F32), low).astype(BF16)
    return vectors * jnp.dot(both, spread, preferred_element_type=F32)


def pair_masks():
    lane = lax.broadcasted_iota(jnp.int32, (1, 2 * LANES), 1)
    for i in range(HEADS // 2):
        masks = []
        for h in (2 * i, 2 * i + 1):
            start = h * HEAD_DIM - i * LANES
            masks.append(jnp.where((lane >= start) & (lane < start + HEAD_DIM), 1.0, 0.0))
        yield i, pl.ds(i * LANES, 2 * LANES), masks


def heads(x_refs, *refs):
    *w_refs, gather_ref, spread_ref, q_gain_ref, k_gain_ref, q_ref, k_ref, v_ref = refs
    _, branch, share, width = x_refs[0].shape
    x = gather_rows(x_refs)
    gather, spread = gather_ref[...], spread_ref[...]

    def product(part):
        return jnp.dot(x, w_refs[part][...], preferred_element_type=F32)

    def per_branch(values):
        values = values.reshape(-1, branch, share, width)
        return [values[:, b].reshape(-1, width) for b in range(branch)]

    def store_pairs(values, gain_ref, ref):
        for b, own in enumerate(per_branch(values)):
            for i, columns, masks in pair_masks():
                for side, mask in enumerate(masks):
                    row = mask if gain_ref is None else mask * gain_ref[:, columns]
                    part = own[:, i * LANES : (i + 2) * LANES]
                    ref[b, i, side] = (part * row).astype(BF16)

    store_pairs(head_scale(product(0), gather, spread), q_gain_ref, q_ref)
    for b, own in enumerate(per_branch(head_scale(product(1), gather, spread))):
        k_ref[b] = (own * k_gain_ref[...]).astype(BF16)
    store_pairs(product(2), None, v_ref)


def head_shapes(xs):
    _, branch, share, width = xs[0].shape
    tokens = sum(x.shape[0] for x in xs) * share
    pairs = (branch, HEADS // 2, 2, tokens, 2 * LANES)
    return [VMEM(shape, BF16) for shape in (pairs, (branch, tokens, width), pairs)]


def heads_kernel(ins, *refs):
    heads(refs[:ins], *refs[ins:])


def early_heads(xs, tables):
    return pl.pallas_call(
        functools.partial(heads_kernel, len(xs)),
        out_shape=head_shapes(xs),
        in_specs=[pl.BlockSpec(memory_space=VMEM)] * (len(xs) + len(tables)),
        out_specs=[pl.BlockSpec(memory_space=VMEM)] * 3,
        compiler_params=params(10),
        name="heads",
    )(*xs, *tables)


def attend_kernel(ins, outs, places, has_early, *refs):
    x_refs, table_refs, refs = refs[:ins], refs[ins : ins + 7], refs[ins + 7 :]
    early, refs = (refs[:3], refs[3:]) if has_early else ((), refs)
    out_refs, late, scores_ref, probs_ref = refs[:outs], refs[outs:-2], refs[-2], refs[-1]
    heads(x_refs, *table_refs, *late)
    _, branch, share, width = x_refs[0].shape
    halves = [early, late] if has_early else [late]
    tokens = sum(half[1].shape[1] for half in halves)
    frames = tokens // share
    same = lax.broadcasted_iota(jnp.int32, (share, 2 * tokens), 0) == lax.rem(
        lax.broadcasted_iota(jnp.int32, (share, 2 * tokens), 1), share
    )

    def rows_of(which, b, i, columns):
        if which == 1:
            return jnp.concatenate([half[1][b, :, columns] for half in halves], axis=0)
        return jnp.concatenate(
            [half[which][b, i, side] for side in range(2) for half in halves], axis=0
        )

    def emit(b, at, block):
        block = block.astype(BF16).reshape(frames // outs, outs, share, LANES)
        for r, out_ref in enumerate(out_refs):
            if places is None:
                out_ref[:, b, :, pl.ds(at, LANES)] = block[:, r]
            else:
                for j, place in enumerate(places):
                    out_ref[place, b, :, pl.ds(at, LANES)] = block[j, r]

    steps = [(i, columns, b) for i, columns, _ in pair_masks() for b in range(branch)]
    carry = [None] * branch

    def score(at):
        i, columns, b = steps[at]
        scores_ref[at] = lax.dot_general(
            rows_of(1, b, i, columns),
            rows_of(0, b, i, columns),
            (((1,), (1,)), ((), ())),
            preferred_element_type=F32,
        )

    def weigh(at):
        scores = scores_ref[at].reshape(frames, share, 2 * tokens)
        top = jnp.max(scores, axis=0)
        weights = jnp.exp2((scores - top) * (HEAD_DIM ** (-0.5) * LOG2_E))
        total = jnp.sum(weights, axis=0)
        probs = weights * jnp.where(same, 1.0 / total, 0.0)
        probs = probs.reshape(tokens, 2 * tokens).astype(BF16)
        probs_ref[at, :tokens] = probs[:, :tokens]
        probs_ref[at, tokens:] = probs[:, tokens:]

    def mix(at):
        i, columns, b = steps[at]
        mixed = lax.dot_general(
            probs_ref[at],
            rows_of(2, b, i, columns),
            (((0,), (0,)), ((), ())),
            preferred_element_type=F32,
        )
        block = mixed[:, :LANES]
        if carry[b] is not None:
            block = block + carry[b]
        carry[b] = mixed[:, LANES:]
        emit(b, i * LANES, block)

    for at in range(len(steps) + 2):
        if at < len(steps):
            score(at)
        if 0 <= at - 1 < len(steps):
            weigh(at - 1)
        if 0 <= at - 2:
            mix(at - 2)
    for b in range(branch):
        emit(b, width - LANES, carry[b])


def attend(xs, tables, early, places, frames, outs):
    _, branch, share, width = xs[0].shape
    tokens = frames * share
    return pl.pallas_call(
        functools.partial(attend_kernel, len(xs), outs, places, bool(early)),
        out_shape=[VMEM((frames // outs, branch, share, width), BF16)] * outs,
        in_specs=[pl.BlockSpec(memory_space=VMEM)] * (len(xs) + len(tables) + len(early)),
        out_specs=[pl.BlockSpec(memory_space=VMEM)] * outs,
        scratch_shapes=[
            *head_shapes(xs),
            VMEM((branch * HEADS // 2, tokens, 2 * tokens), F32),
            VMEM((branch * HEADS // 2, 2 * tokens, tokens), BF16),
        ],
        compiler_params=params(20),
        name="attend",
    )(*xs, *tables, *early)


def project_kernel(exchange, ins, *refs):
    x_refs, (w_ref, gate_ref, residual_ref, out_ref) = refs[:ins], refs[ins:]
    _, branch, share, _ = x_refs[0].shape
    output = jnp.dot(gather_rows(x_refs), w_ref[...], preferred_element_type=F32)
    gated = (gate_ref[...] * output).reshape(-1, branch, share, output.shape[-1])
    for b in range(branch):
        if not exchange:
            out_ref[b] = residual_ref[b] + gated[:, b].reshape(out_ref.shape[1:])
            continue
        for at in range(gated.shape[0]):
            start = pl.multiple_of(block_of(at // 2, at % 2, exchange) * share, share)
            block = pl.ds(start, share)
            out_ref[b, block] = residual_ref[b, block] + gated[at, b]


def project(xs, w_proj, gate_row, rows, exchange):
    branch, patches, width = rows.shape
    cols = 384
    return pl.pallas_call(
        functools.partial(project_kernel, exchange, len(xs)),
        out_shape=jax.ShapeDtypeStruct(rows.shape, F32),
        grid=(width // cols,),
        in_specs=[pl.BlockSpec(x.shape, lambda j: (0, 0, 0, 0)) for x in xs]
        + [
            pl.BlockSpec((width, cols), lambda j: (0, j)),
            pl.BlockSpec((1, cols), lambda j: (0, j)),
            pl.BlockSpec((branch, patches, cols), lambda j: (0, 0, j)),
        ],
        out_specs=pl.BlockSpec((branch, patches, cols), lambda j: (0, 0, j)),
        compiler_params=params(12),
        name="project",
    )(*xs, w_proj, gate_row, rows)


def body(n, exchange, residual, w_qkv, w_proj, q_gain, k_gain, step_mods, timestep):
    rows = residual[:, 0]
    if exchange:
        swap = functools.partial(swap_parts, n)
    else:

        def swap(parts):
            return [lax.all_to_all(parts, "seq", split_axis=0, concat_axis=0, tiled=True)]

    early, places = (), None
    *parts, gate_row = modulate(rows, step_mods, timestep, n, exchange)
    parts = swap(*parts)
    w_first = stage_first(w_qkv, gate_row)
    tables = w_first, *stage_rest(w_qkv, q_gain, k_gain, gate_row)
    if exchange:
        places = (0, *send_order(n))
        first = places[: n // 4]
        early = early_heads([parts[j] for j in first], tables)
        parts = [parts[j] for j in places[n // 4 :]]
    parts = swap(*attend(parts, tables, early, places, n, 2 if exchange else 1))
    return project(parts, w_proj, gate_row, rows, exchange)[:, None]


def solution(mesh):
    in_specs = (P("groups", "seq", None, None), P(), P(), P(), P(), P(), P("groups"))
    out_specs = P("groups", "seq", None, None)
    n = mesh.shape["seq"]

    def step(residual, *others):
        share = residual.shape[2] // n
        exchange = 4 <= n <= 32 and n & (n - 1) == 0 and share % 8 == 0
        run = jax.shard_map(
            functools.partial(body, n, exchange),
            mesh=mesh,
            in_specs=in_specs,
            out_specs=out_specs,
            check_vma=False,
        )
        return run(residual, *others)

    return step
```

```python
import functools

import jax
import jax.numpy as jnp
from jax import lax
from jax.experimental import pallas as pl
from jax.experimental.pallas import tpu as pltpu
from jax.sharding import PartitionSpec as P

HEADS = 16
HEAD_DIM = 72
LANES = 128
LOG2_E = 1.4426950408889634
F32 = jnp.float32
BF16 = jnp.bfloat16
VMEM = pltpu.VMEM


def params(mebibytes):
    return pltpu.CompilerParams(vmem_limit_bytes=mebibytes << 20)


def in_hbm(array):
    return pltpu.with_memory_space_constraint(array, pltpu.HBM)


def block_of(j, r, exchange):
    if not exchange:
        return j
    me = lax.axis_index("seq")
    return jnp.bitwise_xor(me, 2 * j + r)


def modulate_kernel(exchange, step_ref, rows_hbm, mods_hbm, *refs):
    *out_refs, gate_ref, rows_ref, mods_ref, sems = refs
    branch, _, width = rows_ref.shape
    count, _, share, _ = out_refs[0].shape

    def fetch(b):
        return pltpu.make_async_copy(rows_hbm.at[b], rows_ref.at[b], sems.at[b])

    mods = pltpu.make_async_copy(mods_hbm, mods_ref, sems.at[branch])
    fetch(0).start()
    mods.start()
    for b in range(1, branch):
        fetch(b).start()
    mods.wait()
    step = pl.ds(step_ref[0], 1)
    shift_row, scale_row = mods_ref[0, step, :], 1.0 + mods_ref[1, step, :]
    gate_ref[...] = mods_ref[2, step, :]
    group = 1 if exchange else max(1, 32 // share)
    for b in range(branch):
        fetch(b).wait()
        for r, out_ref in enumerate(out_refs):
            for j in range(0, count, group):
                start = block_of(j, r, exchange) * share
                if exchange:
                    start = pl.multiple_of(start, share)
                rows = rows_ref[b, pl.ds(start, group * share)]
                centre = jnp.mean(rows, axis=-1, keepdims=True)
                centred = rows - centre
                variance = jnp.mean(centred * centred, axis=-1, keepdims=True)
                normed = centred * lax.rsqrt(variance + 1e-06) * scale_row + shift_row
                out_ref[j : j + group, b] = normed.reshape(group, share, width).astype(BF16)


def modulate(rows, step_mods, timestep, n, exchange):
    branch, patches, width = rows.shape
    outs = 2 if exchange else 1
    part = VMEM((n // outs, branch, patches // n, width), BF16)
    return pl.pallas_call(
        functools.partial(modulate_kernel, exchange),
        out_shape=[part] * outs + [VMEM((1, width), F32)],
        in_specs=[pl.BlockSpec(memory_space=pltpu.SMEM)] + [pl.BlockSpec(memory_space=pltpu.HBM)] * 2,
        out_specs=[pl.BlockSpec(memory_space=VMEM)] * (outs + 1),
        scratch_shapes=[
            VMEM((branch, patches, width), F32),
            VMEM((3, step_mods.shape[0], width), F32),
            pltpu.SemaphoreType.DMA((branch + 1,)),
        ],
        compiler_params=params(8),
        name="modulate",
    )(timestep, in_hbm(rows), in_hbm(jnp.swapaxes(step_mods, 0, 1)))


def fetch_columns(w_hbm, part, w_ref, sem):
    return pltpu.make_async_copy(
        w_hbm.at[:, pl.ds(part * w_ref.shape[1], w_ref.shape[1])], w_ref, sem
    )


def stage_first_kernel(after_ref, w_hbm, w_ref, sem):
    del after_ref
    copy = fetch_columns(w_hbm, 0, w_ref, sem)
    copy.start()
    copy.wait()


def stage_first(w, after):
    width = w.shape[0]
    return pl.pallas_call(
        stage_first_kernel,
        out_shape=VMEM((width, width), w.dtype),
        in_specs=[pl.BlockSpec(memory_space=VMEM), pl.BlockSpec(memory_space=pltpu.HBM)],
        out_specs=pl.BlockSpec(memory_space=VMEM),
        scratch_shapes=[pltpu.SemaphoreType.DMA],
        compiler_params=params(1),
        name="stage_first",
    )(after, in_hbm(w))


def stage_rest_kernel(after_ref, w_hbm, q_gain_hbm, k_gain_hbm, *refs):
    wk_ref, wv_ref, gather_ref, spread_ref, q_row_ref, k_row_ref, line_ref, sems = refs
    del after_ref
    gains = [
        pltpu.make_async_copy(gain, line_ref.at[at], sems.at[at])
        for at, gain in enumerate((q_gain_hbm, k_gain_hbm))
    ]
    columns = [
        fetch_columns(w_hbm, part, ref, sems.at[part + 1])
        for part, ref in ((1, wk_ref), (2, wv_ref))
    ]
    for copy in gains + columns:
        copy.start()
    gather_ref[...] = head_of(gather_ref.shape, 0)
    spread_ref[...] = head_of(spread_ref.shape, 1)
    for at, row_ref in enumerate((q_row_ref, k_row_ref)):
        gains[at].wait()
        row_ref[...] = line_ref[at].reshape(row_ref.shape)
    for copy in columns:
        copy.wait()


def stage_rest(w, q_gain, k_gain, after):
    width = w.shape[0]
    hbm = pl.BlockSpec(memory_space=pltpu.HBM)
    return pl.pallas_call(
        stage_rest_kernel,
        out_shape=[
            VMEM((width, width), w.dtype),
            VMEM((width, width), w.dtype),
            VMEM((width, LANES), BF16),
            VMEM((LANES, width), BF16),
            VMEM((1, width), F32),
            VMEM((1, width), F32),
        ],
        in_specs=[pl.BlockSpec(memory_space=VMEM), hbm, hbm, hbm],
        out_specs=[pl.BlockSpec(memory_space=VMEM)] * 6,
        scratch_shapes=[VMEM((2, width), F32), pltpu.SemaphoreType.DMA((4,))],
        compiler_params=params(2),
        name="stage_rest",
    )(after, in_hbm(w), in_hbm(q_gain), in_hbm(k_gain))


def pack_kernel(keep_ref, got_ref, *out_refs):
    for j, out_ref in enumerate(out_refs):
        out_ref[0] = keep_ref[j]
        out_ref[1] = got_ref[j]


def pack(keep, got):
    count, *part = keep.shape
    return pl.pallas_call(
        pack_kernel,
        out_shape=[VMEM((2, *part), keep.dtype)] * count,
        in_specs=[pl.BlockSpec(memory_space=VMEM)] * 2,
        out_specs=[pl.BlockSpec(memory_space=VMEM)] * count,
        compiler_params=params(1),
        name="pack",
    )(keep, got)


def send_order(n):
    far, near = [*range(n // 4, n // 2)], [*range(1, n // 4)]
    return [*far[:2], *near[-1:], *far[:1:-1], *near[-2::-1]]


def swap_parts(n, keep, give):
    got = lax.ppermute(give, "seq", [(s, s ^ 1) for s in range(n)])
    parts = list(pack(keep, got))
    for j in send_order(n):
        parts[j] = lax.ppermute(parts[j], "seq", [(s, s ^ (2 * j)) for s in range(n)])
    return parts


def gather_rows(x_refs):
    return jnp.concatenate([ref[...].reshape(-1, ref.shape[-1]) for ref in x_refs], axis=0)


def head_of(shape, feature_dim):
    feature = lax.broadcasted_iota(jnp.int32, shape, feature_dim)
    place = lax.broadcasted_iota(jnp.int32, shape, 1 - feature_dim)
    first = lax.rem(place, HEADS) * HEAD_DIM
    inside = (feature >= first) & (feature < first + HEAD_DIM) & (place < 2 * HEADS)
    return jnp.where(inside, 1.0, 0.0).astype(BF16)


def high_low(wide):
    high = wide.astype(BF16)
    return high, wide - high.astype(F32)


def head_factor(vectors, gather):
    high, low = high_low(vectors * vectors)
    square = jnp.dot(high, gather, preferred_element_type=F32)
    square += jnp.dot(low.astype(BF16), gather, preferred_element_type=F32)
    high, low = high_low(lax.rsqrt(square * (1.0 / HEAD_DIM) + 1e-06))
    place = lax.broadcasted_iota(jnp.int32, low.shape, 1)
    return jnp.where(place < HEADS, high.astype(F32), low).astype(BF16)


def pair_masks():
    lane = lax.broadcasted_iota(jnp.int32, (1, 2 * LANES), 1)
    for i in range(HEADS // 2):
        masks = []
        for h in (2 * i, 2 * i + 1):
            start = h * HEAD_DIM - i * LANES
            masks.append(jnp.where((lane >= start) & (lane < start + HEAD_DIM), 1.0, 0.0))
        yield i, pl.ds(i * LANES, 2 * LANES), masks


def heads(x_refs, *refs):
    *w_refs, gather_ref, spread_ref, q_gain_ref, k_gain_ref, q_ref, k_ref, v_ref, wide_ref = refs
    _, branch, share, width = x_refs[0].shape
    x = gather_rows(x_refs)
    gather, spread = gather_ref[...], spread_ref[...]

    def product(part):
        return jnp.dot(x, w_refs[part][...], preferred_element_type=F32)

    def per_branch(values):
        values = values.reshape(-1, branch, share, width)
        return [values[:, b].reshape(-1, width) for b in range(branch)]

    def store_pairs(values, gain_ref, ref):
        for b, own in enumerate(per_branch(values)):
            for i, columns, masks in pair_masks():
                for side, mask in enumerate(masks):
                    row = mask if gain_ref is None else mask * gain_ref[:, columns]
                    part = own[:, i * LANES : (i + 2) * LANES]
                    ref[b, i, side] = (part * row).astype(BF16)

    def scaled(part, factor):
        return wide_ref[part] * jnp.dot(factor, spread, preferred_element_type=F32)

    wide_ref[0] = product(0)
    wide_ref[1] = product(1)
    q_factor = head_factor(wide_ref[0], gather)
    store_pairs(product(2), None, v_ref)
    k_factor = head_factor(wide_ref[1], gather)
    store_pairs(scaled(0, q_factor), q_gain_ref, q_ref)
    for b, own in enumerate(per_branch(scaled(1, k_factor))):
        k_ref[b] = (own * k_gain_ref[...]).astype(BF16)


def head_shapes(xs):
    _, branch, share, width = xs[0].shape
    tokens = sum(x.shape[0] for x in xs) * share
    pairs = (branch, HEADS // 2, 2, tokens, 2 * LANES)
    return [VMEM(shape, BF16) for shape in (pairs, (branch, tokens, width), pairs)]


def wide_shape(xs):
    _, branch, share, width = xs[0].shape
    return VMEM((2, sum(x.shape[0] for x in xs) * branch * share, width), F32)


def heads_kernel(ins, *refs):
    heads(refs[:ins], *refs[ins:])


def early_heads(xs, tables):
    return pl.pallas_call(
        functools.partial(heads_kernel, len(xs)),
        out_shape=head_shapes(xs),
        in_specs=[pl.BlockSpec(memory_space=VMEM)] * (len(xs) + len(tables)),
        out_specs=[pl.BlockSpec(memory_space=VMEM)] * 3,
        scratch_shapes=[wide_shape(xs)],
        compiler_params=params(10),
        name="heads",
    )(*xs, *tables)


def attend_kernel(ins, outs, places, has_early, *refs):
    x_refs, table_refs, refs = refs[:ins], refs[ins : ins + 7], refs[ins + 7 :]
    early, refs = (refs[:3], refs[3:]) if has_early else ((), refs)
    out_refs, (*late, wide_ref, scores_ref, probs_ref) = refs[:outs], refs[outs:]
    heads(x_refs, *table_refs, *late, wide_ref)
    _, branch, share, width = x_refs[0].shape
    halves = [early, late] if has_early else [late]
    tokens = sum(half[1].shape[1] for half in halves)
    frames = tokens // share
    same = lax.broadcasted_iota(jnp.int32, (share, 2 * tokens), 0) == lax.rem(
        lax.broadcasted_iota(jnp.int32, (share, 2 * tokens), 1), share
    )

    def rows_of(which, b, i, columns):
        if which == 1:
            return jnp.concatenate([half[1][b, :, columns] for half in halves], axis=0)
        return jnp.concatenate(
            [half[which][b, i, side] for side in range(2) for half in halves], axis=0
        )

    def emit(b, at, block):
        block = block.astype(BF16).reshape(frames // outs, outs, share, LANES)
        for r, out_ref in enumerate(out_refs):
            if places is None:
                out_ref[:, b, :, pl.ds(at, LANES)] = block[:, r]
            else:
                for j, place in enumerate(places):
                    out_ref[place, b, :, pl.ds(at, LANES)] = block[j, r]

    steps = [(i, columns, b) for i, columns, _ in pair_masks() for b in range(branch)]
    carry = [None] * branch

    def score(at):
        i, columns, b = steps[at]
        scores_ref[at] = lax.dot_general(
            rows_of(1, b, i, columns),
            rows_of(0, b, i, columns),
            (((1,), (1,)), ((), ())),
            preferred_element_type=F32,
        )

    def weigh(at):
        scores = scores_ref[at].reshape(frames, share, 2 * tokens)
        top = jnp.max(scores, axis=0)
        weights = jnp.exp2((scores - top) * (HEAD_DIM ** (-0.5) * LOG2_E))
        total = jnp.sum(weights, axis=0)
        probs = weights * jnp.where(same, 1.0 / total, 0.0)
        probs = probs.reshape(tokens, 2 * tokens).astype(BF16)
        probs_ref[at, :tokens] = probs[:, :tokens]
        probs_ref[at, tokens:] = probs[:, tokens:]

    def mix(at):
        i, columns, b = steps[at]
        mixed = lax.dot_general(
            probs_ref[at],
            rows_of(2, b, i, columns),
            (((0,), (0,)), ((), ())),
            preferred_element_type=F32,
        )
        block = mixed[:, :LANES]
        if carry[b] is not None:
            block = block + carry[b]
        carry[b] = mixed[:, LANES:]
        emit(b, i * LANES, block)

    for at in range(len(steps) + 2):
        if at < len(steps):
            score(at)
        if 0 <= at - 1 < len(steps):
            weigh(at - 1)
        if 0 <= at - 2:
            mix(at - 2)
    for b in range(branch):
        emit(b, width - LANES, carry[b])


def attend(xs, tables, early, places, frames, outs):
    _, branch, share, width = xs[0].shape
    tokens = frames * share
    return pl.pallas_call(
        functools.partial(attend_kernel, len(xs), outs, places, bool(early)),
        out_shape=[VMEM((frames // outs, branch, share, width), BF16)] * outs,
        in_specs=[pl.BlockSpec(memory_space=VMEM)] * (len(xs) + len(tables) + len(early)),
        out_specs=[pl.BlockSpec(memory_space=VMEM)] * outs,
        scratch_shapes=[
            *head_shapes(xs),
            wide_shape(xs),
            VMEM((branch * HEADS // 2, tokens, 2 * tokens), F32),
            VMEM((branch * HEADS // 2, 2 * tokens, tokens), BF16),
        ],
        compiler_params=params(20),
        name="attend",
    )(*xs, *tables, *early)


def project_kernel(ins, *refs):
    x_refs, (w_ref, gate_ref, residual_ref, out_ref) = refs[:ins], refs[ins:]
    _, branch, share, _ = x_refs[0].shape
    output = jnp.dot(gather_rows(x_refs), w_ref[...], preferred_element_type=F32)
    gated = (gate_ref[...] * output).reshape(-1, branch, share, output.shape[-1])
    for b in range(branch):
        out_ref[b] = residual_ref[b] + gated[:, b].reshape(out_ref.shape[1:])


def project(xs, w_proj, gate_row, rows):
    branch, patches, width = rows.shape
    cols = 384
    return pl.pallas_call(
        functools.partial(project_kernel, len(xs)),
        out_shape=jax.ShapeDtypeStruct(rows.shape, F32),
        grid=(width // cols,),
        in_specs=[pl.BlockSpec(x.shape, lambda j: (0, 0, 0, 0)) for x in xs]
        + [
            pl.BlockSpec((width, cols), lambda j: (0, j)),
            pl.BlockSpec((1, cols), lambda j: (0, j)),
            pl.BlockSpec((branch, patches, cols), lambda j: (0, 0, j)),
        ],
        out_specs=pl.BlockSpec((branch, patches, cols), lambda j: (0, 0, j)),
        compiler_params=params(12),
        name="project",
    )(*xs, w_proj, gate_row, rows)


def project_part_kernel(places, *refs):
    ins = len(places)
    x_refs, (w_ref, gate_ref, residual_ref) = refs[:ins], refs[ins : ins + 3]
    out_hbm, buffer_ref, sems = refs[-3:]
    _, branch, share, width = x_refs[0].shape
    x = gather_rows(x_refs)
    core = lax.rem(lax.axis_index("seq"), 2)
    cols = width // 3
    copies = []
    for at in range(0, width, cols):
        columns = pl.ds(at, cols)
        output = jnp.dot(x, w_ref[:, columns], preferred_element_type=F32)
        gated = (gate_ref[:, columns] * output).reshape(ins, 2, branch, share, cols)
        for slot, j in enumerate(places):
            start = pl.multiple_of((block_of(j, 0, True) - core) * share, 2 * share)
            for b in range(branch):
                for r in range(2):
                    own = pl.multiple_of(jnp.bitwise_xor(core, r) * share, share)
                    block = pl.ds(pl.multiple_of(start + own, share), share)
                    buffer_ref[slot, b, pl.ds(own, share), columns] = (
                        residual_ref[b, block, columns] + gated[slot, r, b]
                    )
                copies.append(
                    pltpu.make_async_copy(
                        buffer_ref.at[slot, b, :, columns],
                        out_hbm.at[b, pl.ds(start, 2 * share), columns],
                        sems.at[len(copies)],
                    )
                )
                copies[-1].start()
    for copy in copies:
        copy.wait()


def project_part(xs, places, w_proj, gate_row, rows, before):
    branch, _, width = rows.shape
    share = xs[0].shape[2]
    hbm = pl.BlockSpec(memory_space=pltpu.HBM)
    return pl.pallas_call(
        functools.partial(project_part_kernel, places),
        out_shape=pltpu.HBM(rows.shape, F32),
        in_specs=[pl.BlockSpec(memory_space=VMEM)] * (len(xs) + 3) + [hbm] * len(before),
        out_specs=hbm,
        scratch_shapes=[
            VMEM((len(xs), branch, 2 * share, width), F32),
            pltpu.SemaphoreType.DMA((3 * branch * len(xs),)),
        ],
        input_output_aliases={len(xs) + 3: 0} if before else {},
        compiler_params=params(6),
        name="project",
    )(*xs, w_proj, gate_row, rows, *before)


def body(n, exchange, residual, w_qkv, w_proj, q_gain, k_gain, step_mods, timestep):
    rows = residual[:, 0]
    if exchange:
        swap = functools.partial(swap_parts, n)
    else:

        def swap(parts):
            return [lax.all_to_all(parts, "seq", split_axis=0, concat_axis=0, tiled=True)]

    early, places = (), None
    *parts, gate_row = modulate(rows, step_mods, timestep, n, exchange)
    parts = swap(*parts)
    w_first = stage_first(w_qkv, gate_row)
    tables = w_first, *stage_rest(w_qkv, q_gain, k_gain, gate_row)
    if exchange:
        places = (0, *send_order(n))
        first = places[: n // 4]
        early = early_heads([parts[j] for j in first], tables)
        parts = [parts[j] for j in places[n // 4 :]]
    parts = swap(*attend(parts, tables, early, places, n, 2 if exchange else 1))
    if not exchange:
        return project(parts, w_proj, gate_row, rows)[:, None]
    out = []
    for part in (places[: n // 4], places[n // 4 :]):
        own = [parts[j] for j in part]
        out = [project_part(own, part, w_proj, gate_row, rows, out)]
    return out[0][:, None]


def solution(mesh):
    in_specs = (P("groups", "seq", None, None), P(), P(), P(), P(), P(), P("groups"))
    out_specs = P("groups", "seq", None, None)
    n = mesh.shape["seq"]

    def step(residual, *others):
        share = residual.shape[2] // n
        exchange = 4 <= n <= 32 and n & (n - 1) == 0 and share % 8 == 0
        run = jax.shard_map(
            functools.partial(body, n, exchange),
            mesh=mesh,
            in_specs=in_specs,
            out_specs=out_specs,
            check_vma=False,
        )
        return run(residual, *others)

    return step
```

```python
import functools

import jax
import jax.numpy as jnp
from jax import lax
from jax.experimental import pallas as pl
from jax.experimental.pallas import tpu as pltpu
from jax.sharding import PartitionSpec as P

HEADS = 16
HEAD_DIM = 72
LANES = 128
LOG2_E = 1.4426950408889634
F32 = jnp.float32
BF16 = jnp.bfloat16
VMEM = pltpu.VMEM


def params(mebibytes):
    return pltpu.CompilerParams(vmem_limit_bytes=mebibytes << 20)


def in_hbm(array):
    return pltpu.with_memory_space_constraint(array, pltpu.HBM)


def block_of(j, r, exchange):
    if not exchange:
        return j
    me = lax.axis_index("seq")
    return jnp.bitwise_xor(me, 2 * j + r)


def modulate_rows(rows_ref, scale_row, shift_row, out_ref, r, exchange, branches):
    count, _, share, width = out_ref.shape
    group = 1 if exchange else max(1, 32 // share)
    for b in branches:
        for j in range(0, count, group):
            start = block_of(j, r, exchange) * share
            if exchange:
                start = pl.multiple_of(start, share)
            rows = rows_ref[b, pl.ds(start, group * share)]
            centre = jnp.mean(rows, axis=-1, keepdims=True)
            centred = rows - centre
            variance = jnp.mean(centred * centred, axis=-1, keepdims=True)
            normed = centred * lax.rsqrt(variance + 1e-06) * scale_row + shift_row
            out_ref[j : j + group, b] = normed.reshape(group, share, width).astype(BF16)


def modulate_kernel(exchange, step_ref, rows_hbm, mods_hbm, out_ref, *refs):
    scale_ref, shift_ref, gate_ref, rows_ref, mods_ref, sems = refs
    branch = rows_ref.shape[0]

    def fetch(b):
        return pltpu.make_async_copy(rows_hbm.at[b], rows_ref.at[b], sems.at[b])

    mods = pltpu.make_async_copy(mods_hbm, mods_ref, sems.at[branch])
    fetch(0).start()
    mods.start()
    for b in range(1, branch):
        fetch(b).start()
    mods.wait()
    step = pl.ds(step_ref[0], 1)
    shift_row, scale_row = mods_ref[0, step, :], 1.0 + mods_ref[1, step, :]
    shift_ref[...] = shift_row
    scale_ref[...] = scale_row
    gate_ref[...] = mods_ref[2, step, :]
    for b in range(branch):
        fetch(b).wait()
        modulate_rows(rows_ref, scale_row, shift_row, out_ref, 1, exchange, [b])


def modulate(rows, step_mods, timestep, n, exchange):
    branch, patches, width = rows.shape
    outs = 2 if exchange else 1
    row = VMEM((1, width), F32)
    return pl.pallas_call(
        functools.partial(modulate_kernel, exchange),
        out_shape=[
            VMEM((n // outs, branch, patches // n, width), BF16),
            row,
            row,
            row,
            VMEM((branch, patches, width), F32),
        ],
        in_specs=[pl.BlockSpec(memory_space=pltpu.SMEM)]
        + [pl.BlockSpec(memory_space=pltpu.HBM)] * 2,
        out_specs=[pl.BlockSpec(memory_space=VMEM)] * 5,
        scratch_shapes=[
            VMEM((3, step_mods.shape[0], width), F32),
            pltpu.SemaphoreType.DMA((branch + 1,)),
        ],
        compiler_params=params(8),
        name="modulate",
    )(timestep, in_hbm(rows), in_hbm(jnp.swapaxes(step_mods, 0, 1)))


def keep_kernel(rows_ref, scale_ref, shift_ref, out_ref):
    branches = range(rows_ref.shape[0])
    modulate_rows(rows_ref, scale_ref[...], shift_ref[...], out_ref, 0, True, branches)


def modulate_kept(rows, scale_row, shift_row, like):
    return pl.pallas_call(
        keep_kernel,
        out_shape=VMEM(like.shape, BF16),
        in_specs=[pl.BlockSpec(memory_space=VMEM)] * 3,
        out_specs=pl.BlockSpec(memory_space=VMEM),
        compiler_params=params(4),
        name="keep",
    )(rows, scale_row, shift_row)


def tables_kernel(after_ref, q_gain_hbm, k_gain_hbm, *refs):
    gather_ref, spread_ref, q_row_ref, k_row_ref, line_ref, sems = refs
    del after_ref
    gains = [
        pltpu.make_async_copy(gain, line_ref.at[at], sems.at[at])
        for at, gain in enumerate((q_gain_hbm, k_gain_hbm))
    ]
    for copy in gains:
        copy.start()
    gather_ref[...] = head_of(gather_ref.shape, 0)
    spread_ref[...] = head_of(spread_ref.shape, 1)
    for at, row_ref in enumerate((q_row_ref, k_row_ref)):
        gains[at].wait()
        row_ref[...] = line_ref[at].reshape(row_ref.shape)


def make_tables(q_gain, k_gain, after):
    width = q_gain.shape[0]
    hbm = pl.BlockSpec(memory_space=pltpu.HBM)
    return pl.pallas_call(
        tables_kernel,
        out_shape=[
            VMEM((width, LANES), BF16),
            VMEM((LANES, width), BF16),
            VMEM((1, width), F32),
            VMEM((1, width), F32),
        ],
        in_specs=[pl.BlockSpec(memory_space=VMEM), hbm, hbm],
        out_specs=[pl.BlockSpec(memory_space=VMEM)] * 4,
        scratch_shapes=[VMEM((2, width), F32), pltpu.SemaphoreType.DMA((2,))],
        compiler_params=params(2),
        name="tables",
    )(after, in_hbm(q_gain), in_hbm(k_gain))


def pack_kernel(keep_ref, got_ref, *out_refs):
    for j, out_ref in enumerate(out_refs):
        out_ref[0] = keep_ref[j]
        out_ref[1] = got_ref[j]


def pack(keep, got):
    count, *part = keep.shape
    return pl.pallas_call(
        pack_kernel,
        out_shape=[VMEM((2, *part), keep.dtype)] * count,
        in_specs=[pl.BlockSpec(memory_space=VMEM)] * 2,
        out_specs=[pl.BlockSpec(memory_space=VMEM)] * count,
        compiler_params=params(1),
        cost_estimate=pl.CostEstimate(flops=10**10, bytes_accessed=10**7, transcendentals=0),
        name="pack",
    )(keep, got)


def send_order(n):
    far, near = [*range(n // 4, n // 2)], [*range(1, n // 4)]
    return [*far[:2], *near[-1:], *far[:1:-1], *near[-2::-1]]


def swap_parts(n, give, make_keep):
    got = lax.ppermute(give, "seq", [(s, s ^ 1) for s in range(n)])
    keep = make_keep()
    parts = list(pack(keep, got))
    for j in send_order(n):
        parts[j] = lax.ppermute(parts[j], "seq", [(s, s ^ (2 * j)) for s in range(n)])
    return parts


def gather_rows(x_refs):
    return jnp.concatenate([ref[...].reshape(-1, ref.shape[-1]) for ref in x_refs], axis=0)


def head_of(shape, feature_dim):
    feature = lax.broadcasted_iota(jnp.int32, shape, feature_dim)
    place = lax.broadcasted_iota(jnp.int32, shape, 1 - feature_dim)
    first = lax.rem(place, HEADS) * HEAD_DIM
    inside = (feature >= first) & (feature < first + HEAD_DIM) & (place < 2 * HEADS)
    return jnp.where(inside, 1.0, 0.0).astype(BF16)


def high_low(wide):
    high = wide.astype(BF16)
    return high, wide - high.astype(F32)


def head_factors(vectors, gather):
    high, low = high_low(vectors * vectors)
    rows = vectors.shape[0]
    stacked = jnp.concatenate([high, low.astype(BF16)], axis=0)
    square = jnp.dot(stacked, gather, preferred_element_type=F32)
    square = square[:rows] + square[rows:]
    high, low = high_low(lax.rsqrt(square * (1.0 / HEAD_DIM) + 1e-06))
    place = lax.broadcasted_iota(jnp.int32, low.shape, 1)
    return jnp.where(place < HEADS, high.astype(F32), low).astype(BF16)


def pair_masks():
    lane = lax.broadcasted_iota(jnp.int32, (1, 2 * LANES), 1)
    for i in range(HEADS // 2):
        masks = []
        for h in (2 * i, 2 * i + 1):
            start = h * HEAD_DIM - i * LANES
            masks.append(jnp.where((lane >= start) & (lane < start + HEAD_DIM), 1.0, 0.0))
        yield i, pl.ds(i * LANES, 2 * LANES), masks


def heads(x_refs, outs, *refs):
    w_ref, gather_ref, spread_ref, q_gain_ref, k_gain_ref, q_ref, k_ref, v_ref, wide_ref = refs
    _, branch, share, width = x_refs[0].shape
    x = gather_rows(x_refs)
    rows = x.shape[0]

    def product(part):
        columns = w_ref[:, part * width : (part + 1) * width]
        return jnp.dot(x, columns, preferred_element_type=F32)

    def per_branch(values):
        values = values.reshape(-1, branch, share, width)
        return [values[:, b].reshape(-1, width) for b in range(branch)]

    wide_ref[:rows] = product(0)
    wide_ref[rows:] = product(1)
    factors = head_factors(wide_ref[...], gather_ref[...])
    for b, own in enumerate(per_branch(product(2))):
        v_ref[b] = own.astype(BF16)
    wide_ref[...] *= jnp.dot(factors, spread_ref[...], preferred_element_type=F32)
    for b, own in enumerate(per_branch(wide_ref[:rows])):
        own = own.reshape(-1, outs, share, width)
        for r in range(outs):
            mine = own[:, r].reshape(-1, width)
            for i, columns, masks in pair_masks():
                part = mine[:, i * LANES : (i + 2) * LANES]
                for side, mask in enumerate(masks):
                    gain = mask * q_gain_ref[:, columns]
                    q_ref[r, b, i, side] = (part * gain).astype(BF16)
    for b, own in enumerate(per_branch(wide_ref[rows:])):
        k_ref[b] = (own * k_gain_ref[...]).astype(BF16)


def head_shapes(xs, outs):
    _, branch, share, width = xs[0].shape
    tokens = sum(x.shape[0] for x in xs) * share
    queries = (outs, branch, HEADS // 2, 2, tokens // outs, 2 * LANES)
    return [VMEM(shape, BF16) for shape in (queries, *[(branch, tokens, width)] * 2)]


def wide_shape(xs):
    _, branch, share, width = xs[0].shape
    return VMEM((2 * sum(x.shape[0] for x in xs) * branch * share, width), F32)


def heads_kernel(ins, outs, *refs):
    heads(refs[:ins], outs, *refs[ins:])


def make_heads(xs, tables, outs):
    return pl.pallas_call(
        functools.partial(heads_kernel, len(xs), outs),
        out_shape=head_shapes(xs, outs),
        in_specs=[pl.BlockSpec(memory_space=VMEM)] * (len(xs) + len(tables)),
        out_specs=[pl.BlockSpec(memory_space=VMEM)] * 3,
        scratch_shapes=[wide_shape(xs)],
        compiler_params=params(10),
        name="heads",
    )(*xs, *tables)


def attend_kernel(r, places, share, *refs):
    *in_refs, out_ref, scores_ref, probs_ref = refs
    groups = [in_refs[at : at + 3] for at in range(0, len(in_refs), 3)]
    _, branch, tokens, queries = scores_ref.shape[0], *out_ref.shape[1:2], *scores_ref.shape[1:]
    frames = tokens // share
    width = out_ref.shape[-1]
    same = lax.broadcasted_iota(jnp.int32, (share, queries), 0) == lax.rem(
        lax.broadcasted_iota(jnp.int32, (share, queries), 1), share
    )

    def rows_of(which, b, columns):
        return jnp.concatenate([group[which][b, :, columns] for group in groups], axis=0)

    def queries_of(b, i):
        return jnp.concatenate(
            [group[0][r, b, i, side] for side in range(2) for group in groups], axis=0
        )

    def emit(b, at, block):
        block = block.astype(BF16).reshape(-1, share, LANES)
        if places is None:
            out_ref[:, b, :, pl.ds(at, LANES)] = block
            return
        for slot, place in enumerate(places):
            out_ref[place, b, :, pl.ds(at, LANES)] = block[slot]

    steps = [(i, columns, masks, b) for i, columns, masks in pair_masks() for b in range(branch)]
    carry = [None] * branch

    def score(at):
        i, columns, _, b = steps[at]
        scores_ref[at] = lax.dot_general(
            rows_of(1, b, columns),
            queries_of(b, i),
            (((1,), (1,)), ((), ())),
            preferred_element_type=F32,
        )

    def weigh(at):
        scores = scores_ref[at].reshape(frames, share, queries)
        top = jnp.max(scores, axis=0)
        weights = jnp.exp2((scores - top) * (HEAD_DIM ** (-0.5) * LOG2_E))
        total = jnp.sum(weights, axis=0)
        probs = weights * jnp.where(same, 1.0 / total, 0.0)
        probs_ref[at] = probs.reshape(tokens, queries).astype(BF16)

    def mix(at):
        i, columns, masks, b = steps[at]
        mixed = lax.dot_general(
            probs_ref[at],
            rows_of(2, b, columns),
            (((0,), (0,)), ((), ())),
            preferred_element_type=F32,
        )
        half = queries // 2
        mixed = jnp.where(
            masks[0] > 0.0, mixed[:half], jnp.where(masks[1] > 0.0, mixed[half:], 0.0)
        )
        block = mixed[:, :LANES]
        if carry[b] is not None:
            block = block + carry[b]
        carry[b] = mixed[:, LANES:]
        emit(b, i * LANES, block)

    for at in range(len(steps) + 2):
        if at < len(steps):
            score(at)
        if 0 <= at - 1 < len(steps):
            weigh(at - 1)
        if 0 <= at - 2:
            mix(at - 2)
    for b in range(branch):
        emit(b, width - LANES, carry[b])


def attend(r, groups, places, frames, share, outs):
    branch, _, width = groups[0][1].shape
    tokens = frames * share
    steps, queries = branch * HEADS // 2, 2 * tokens // outs
    flat = [array for group in groups for array in group]
    return pl.pallas_call(
        functools.partial(attend_kernel, r, places, share),
        out_shape=VMEM((frames // outs, branch, share, width), BF16),
        in_specs=[pl.BlockSpec(memory_space=VMEM)] * len(flat),
        out_specs=pl.BlockSpec(memory_space=VMEM),
        scratch_shapes=[
            VMEM((steps, tokens, queries), F32),
            VMEM((steps, tokens, queries), BF16),
        ],
        compiler_params=params(10),
        name="attend",
    )(*flat)


def project_kernel(ins, *refs):
    x_refs, (w_ref, gate_ref, residual_ref, out_ref) = refs[:ins], refs[ins:]
    _, branch, share, _ = x_refs[0].shape
    output = jnp.dot(gather_rows(x_refs), w_ref[...], preferred_element_type=F32)
    gated = (gate_ref[...] * output).reshape(-1, branch, share, output.shape[-1])
    for b in range(branch):
        out_ref[b] = residual_ref[b] + gated[:, b].reshape(out_ref.shape[1:])


def project(xs, w_proj, gate_row, rows):
    branch, patches, width = rows.shape
    cols = 384
    return pl.pallas_call(
        functools.partial(project_kernel, len(xs)),
        out_shape=jax.ShapeDtypeStruct(rows.shape, F32),
        grid=(width // cols,),
        in_specs=[pl.BlockSpec(x.shape, lambda j: (0, 0, 0, 0)) for x in xs]
        + [
            pl.BlockSpec((width, cols), lambda j: (0, j)),
            pl.BlockSpec((1, cols), lambda j: (0, j)),
            pl.BlockSpec((branch, patches, cols), lambda j: (0, 0, j)),
        ],
        out_specs=pl.BlockSpec((branch, patches, cols), lambda j: (0, 0, j)),
        compiler_params=params(12),
        name="project",
    )(*xs, w_proj, gate_row, rows)


def project_part_kernel(places, *refs):
    ins = len(places)
    x_refs, (w_ref, gate_ref, residual_ref) = refs[:ins], refs[ins : ins + 3]
    out_hbm, buffer_ref, sems = refs[-3:]
    _, branch, share, width = x_refs[0].shape
    x = gather_rows(x_refs)
    core = lax.rem(lax.axis_index("seq"), 2)
    cols = width // 3
    copies = []
    for at in range(0, width, cols):
        columns = pl.ds(at, cols)
        output = jnp.dot(x, w_ref[:, columns], preferred_element_type=F32)
        gated = (gate_ref[:, columns] * output).reshape(ins, 2, branch, share, cols)
        for slot, j in enumerate(places):
            start = pl.multiple_of((block_of(j, 0, True) - core) * share, 2 * share)
            for b in range(branch):
                for r in range(2):
                    own = pl.multiple_of(jnp.bitwise_xor(core, r) * share, share)
                    block = pl.ds(pl.multiple_of(start + own, share), share)
                    buffer_ref[slot, b, pl.ds(own, share), columns] = (
                        residual_ref[b, block, columns] + gated[slot, r, b]
                    )
                copies.append(
                    pltpu.make_async_copy(
                        buffer_ref.at[slot, b, :, columns],
                        out_hbm.at[b, pl.ds(start, 2 * share), columns],
                        sems.at[len(copies)],
                    )
                )
                copies[-1].start()
    for copy in copies:
        copy.wait()


def project_part(xs, places, w_proj, gate_row, rows, before):
    branch, _, width = rows.shape
    share = xs[0].shape[2]
    hbm = pl.BlockSpec(memory_space=pltpu.HBM)
    return pl.pallas_call(
        functools.partial(project_part_kernel, places),
        out_shape=pltpu.HBM(rows.shape, F32),
        in_specs=[pl.BlockSpec(memory_space=VMEM)] * (len(xs) + 3) + [hbm] * len(before),
        out_specs=hbm,
        scratch_shapes=[
            VMEM((len(xs), branch, 2 * share, width), F32),
            pltpu.SemaphoreType.DMA((3 * branch * len(xs),)),
        ],
        input_output_aliases={len(xs) + 3: 0} if before else {},
        compiler_params=params(6),
        name="project",
    )(*xs, w_proj, gate_row, rows, *before)


def body(n, exchange, residual, w_qkv, w_proj, q_gain, k_gain, step_mods, timestep):
    rows = residual[:, 0]
    share = rows.shape[1] // n
    if not exchange:
        swap = functools.partial(
            lax.all_to_all, axis_name="seq", split_axis=0, concat_axis=0, tiled=True
        )
        parts, *_, gate_row, _ = modulate(rows, step_mods, timestep, n, exchange)
        tables = w_qkv, *make_tables(q_gain, k_gain, gate_row)
        group = make_heads([swap(parts)], tables, 1)
        attended = swap(attend(0, [group], None, n, share, 1))
        return project([attended], w_proj, gate_row, rows)[:, None]

    places = (0, *send_order(n))
    first, last = places[: n // 4], places[n // 4 :]
    give, scale_row, shift_row, gate_row, held = modulate(rows, step_mods, timestep, n, exchange)
    parts = swap_parts(n, give, lambda: modulate_kept(held, scale_row, shift_row, give))
    tables = w_qkv, *make_tables(q_gain, k_gain, gate_row)
    early = make_heads([parts[j] for j in first], tables, 2)
    groups = early, make_heads([parts[j] for j in last], tables, 2)
    give = attend(1, groups, places, n, share, 2)
    parts = swap_parts(n, give, lambda: attend(0, groups, places, n, share, 2))
    out = []
    for part in (first, last):
        own = [parts[j] for j in part]
        out = [project_part(own, part, w_proj, gate_row, rows, out)]
    return out[0][:, None]


def solution(mesh):
    in_specs = (P("groups", "seq", None, None), P(), P(), P(), P(), P(), P("groups"))
    out_specs = P("groups", "seq", None, None)
    n = mesh.shape["seq"]

    def step(residual, *others):
        share = residual.shape[2] // n
        exchange = 4 <= n <= 32 and n & (n - 1) == 0 and share % 8 == 0
        run = jax.shard_map(
            functools.partial(body, n, exchange),
            mesh=mesh,
            in_specs=in_specs,
            out_specs=out_specs,
            check_vma=False,
        )
        return run(residual, *others)

    return step
```

```python
import functools

import jax
import jax.numpy as jnp
from jax import lax
from jax.experimental import pallas as pl
from jax.experimental.pallas import tpu as pltpu
from jax.sharding import PartitionSpec as P

HEADS = 16
HEAD_DIM = 72
LANES = 128
LOG2_E = 1.4426950408889634
F32 = jnp.float32
BF16 = jnp.bfloat16
VMEM = pltpu.VMEM


def params(mebibytes):
    return pltpu.CompilerParams(vmem_limit_bytes=mebibytes << 20)


def in_hbm(array):
    return pltpu.with_memory_space_constraint(array, pltpu.HBM)


def block_of(j, r, exchange):
    if not exchange:
        return j
    me = lax.axis_index("seq")
    return jnp.bitwise_xor(me, 2 * j + r)


def modulate_rows(rows_ref, scale_row, shift_row, out_ref, r, exchange, branches):
    count, _, share, width = out_ref.shape
    group = 1 if exchange else max(1, 32 // share)
    for b in branches:
        for j in range(0, count, group):
            start = block_of(j, r, exchange) * share
            if exchange:
                start = pl.multiple_of(start, share)
            rows = rows_ref[b, pl.ds(start, group * share)]
            centre = jnp.mean(rows, axis=-1, keepdims=True)
            centred = rows - centre
            variance = jnp.mean(centred * centred, axis=-1, keepdims=True)
            normed = centred * lax.rsqrt(variance + 1e-06) * scale_row + shift_row
            out_ref[j : j + group, b] = normed.reshape(group, share, width).astype(BF16)


def modulate_kernel(exchange, step_ref, rows_hbm, mods_hbm, out_ref, *refs):
    scale_ref, shift_ref, gate_ref, rows_ref, mods_ref, sems = refs
    branch = rows_ref.shape[0]

    def fetch(b):
        return pltpu.make_async_copy(rows_hbm.at[b], rows_ref.at[b], sems.at[b])

    mods = pltpu.make_async_copy(mods_hbm, mods_ref, sems.at[branch])
    fetch(0).start()
    mods.start()
    for b in range(1, branch):
        fetch(b).start()
    mods.wait()
    step = pl.ds(step_ref[0], 1)
    shift_row, scale_row = mods_ref[0, step, :], 1.0 + mods_ref[1, step, :]
    shift_ref[...] = shift_row
    scale_ref[...] = scale_row
    gate_ref[...] = mods_ref[2, step, :]
    for b in range(branch):
        fetch(b).wait()
        modulate_rows(rows_ref, scale_row, shift_row, out_ref, 1, exchange, [b])


def modulate(rows, step_mods, timestep, n, exchange):
    branch, patches, width = rows.shape
    outs = 2 if exchange else 1
    row = VMEM((1, width), F32)
    return pl.pallas_call(
        functools.partial(modulate_kernel, exchange),
        out_shape=[
            VMEM((n // outs, branch, patches // n, width), BF16),
            row,
            row,
            row,
            VMEM((branch, patches, width), F32),
        ],
        in_specs=[pl.BlockSpec(memory_space=pltpu.SMEM)]
        + [pl.BlockSpec(memory_space=pltpu.HBM)] * 2,
        out_specs=[pl.BlockSpec(memory_space=VMEM)] * 5,
        scratch_shapes=[
            VMEM((3, step_mods.shape[0], width), F32),
            pltpu.SemaphoreType.DMA((branch + 1,)),
        ],
        compiler_params=params(8),
        name="modulate",
    )(timestep, in_hbm(rows), in_hbm(jnp.swapaxes(step_mods, 0, 1)))


def keep_kernel(lead, rows_ref, scale_ref, shift_ref, out_ref, lead_ref):
    branches = range(rows_ref.shape[0])
    modulate_rows(rows_ref, scale_ref[...], shift_ref[...], out_ref, 0, True, branches)
    lead_ref[0] = out_ref[lead]


def modulate_kept(rows, scale_row, shift_row, like, lead):
    return pl.pallas_call(
        functools.partial(keep_kernel, lead),
        out_shape=[VMEM(like.shape, BF16), VMEM((1, *like.shape[1:]), BF16)],
        in_specs=[pl.BlockSpec(memory_space=VMEM)] * 3,
        out_specs=[pl.BlockSpec(memory_space=VMEM)] * 2,
        compiler_params=params(4),
        name="keep",
    )(rows, scale_row, shift_row)


def tables_kernel(after_ref, q_gain_hbm, k_gain_hbm, *refs):
    gather_ref, spread_ref, q_row_ref, k_row_ref, line_ref, sems = refs
    del after_ref
    gains = [
        pltpu.make_async_copy(gain, line_ref.at[at], sems.at[at])
        for at, gain in enumerate((q_gain_hbm, k_gain_hbm))
    ]
    for copy in gains:
        copy.start()
    gather_ref[...] = head_of(gather_ref.shape, 0)
    spread_ref[...] = head_of(spread_ref.shape, 1)
    for at, row_ref in enumerate((q_row_ref, k_row_ref)):
        gains[at].wait()
        row_ref[...] = line_ref[at].reshape(row_ref.shape)


def make_tables(q_gain, k_gain, after):
    width = q_gain.shape[0]
    hbm = pl.BlockSpec(memory_space=pltpu.HBM)
    return pl.pallas_call(
        tables_kernel,
        out_shape=[
            VMEM((width, LANES), BF16),
            VMEM((LANES, width), BF16),
            VMEM((1, width), F32),
            VMEM((1, width), F32),
        ],
        in_specs=[pl.BlockSpec(memory_space=VMEM), hbm, hbm],
        out_specs=[pl.BlockSpec(memory_space=VMEM)] * 4,
        scratch_shapes=[VMEM((2, width), F32), pltpu.SemaphoreType.DMA((2,))],
        compiler_params=params(2),
        name="tables",
    )(after, in_hbm(q_gain), in_hbm(k_gain))


def pack_kernel(lead, keep_ref, got_ref, *out_refs):
    for j, out_ref in enumerate(out_refs):
        if j == lead:
            out_ref[0] = got_ref[j]
        else:
            out_ref[0] = keep_ref[j]
            out_ref[1] = got_ref[j]


def pack(keep, got, lead):
    count, *part = keep.shape
    return pl.pallas_call(
        functools.partial(pack_kernel, lead),
        out_shape=[VMEM((1 if j == lead else 2, *part), keep.dtype) for j in range(count)],
        in_specs=[pl.BlockSpec(memory_space=VMEM)] * 2,
        out_specs=[pl.BlockSpec(memory_space=VMEM)] * count,
        compiler_params=params(1),
        cost_estimate=pl.CostEstimate(flops=10**10, bytes_accessed=10**7, transcendentals=0),
        name="pack",
    )(keep, got)


def send_order(n):
    far, near = [*range(n // 4, n // 2)], [*range(1, n // 4)]
    return [*far[:2], *near[-1:], *far[:1:-1], *near[-2::-1]]


def swap_parts(n, give, make_keep):
    def send(j, part):
        return lax.ppermute(part, "seq", [(s, s ^ (2 * j)) for s in range(n)])

    order = send_order(n)
    got = lax.ppermute(give, "seq", [(s, s ^ 1) for s in range(n)])
    keep, first = make_keep()
    first = send(order[0], first)
    parts = [[part] for part in pack(keep, got, order[0])]
    for j in order:
        parts[j] = [send(j, parts[j][0])]
    parts[order[0]].insert(0, first)
    return parts


def gather_rows(x_refs):
    return jnp.concatenate([ref[...].reshape(-1, ref.shape[-1]) for ref in x_refs], axis=0)


def head_of(shape, feature_dim):
    feature = lax.broadcasted_iota(jnp.int32, shape, feature_dim)
    place = lax.broadcasted_iota(jnp.int32, shape, 1 - feature_dim)
    first = lax.rem(place, HEADS) * HEAD_DIM
    inside = (feature >= first) & (feature < first + HEAD_DIM) & (place < 2 * HEADS)
    return jnp.where(inside, 1.0, 0.0).astype(BF16)


def high_low(wide):
    high = wide.astype(BF16)
    return high, wide - high.astype(F32)


def head_factors(vectors, gather):
    high, low = high_low(vectors * vectors)
    rows = vectors.shape[0]
    stacked = jnp.concatenate([high, low.astype(BF16)], axis=0)
    square = jnp.dot(stacked, gather, preferred_element_type=F32)
    square = square[:rows] + square[rows:]
    high, low = high_low(lax.rsqrt(square * (1.0 / HEAD_DIM) + 1e-06))
    place = lax.broadcasted_iota(jnp.int32, low.shape, 1)
    return jnp.where(place < HEADS, high.astype(F32), low).astype(BF16)


def pair_masks():
    lane = lax.broadcasted_iota(jnp.int32, (1, 2 * LANES), 1)
    for i in range(HEADS // 2):
        masks = []
        for h in (2 * i, 2 * i + 1):
            start = h * HEAD_DIM - i * LANES
            masks.append(jnp.where((lane >= start) & (lane < start + HEAD_DIM), 1.0, 0.0))
        yield i, pl.ds(i * LANES, 2 * LANES), masks


def heads(x_refs, outs, *refs):
    w_ref, gather_ref, spread_ref, q_gain_ref, k_gain_ref, q_ref, k_ref, v_ref, wide_ref = refs
    _, branch, share, width = x_refs[0].shape
    x = gather_rows(x_refs)
    rows = x.shape[0]

    def product(part):
        columns = w_ref[:, part * width : (part + 1) * width]
        return jnp.dot(x, columns, preferred_element_type=F32)

    def per_branch(values):
        values = values.reshape(-1, branch, share, width)
        return [values[:, b].reshape(-1, width) for b in range(branch)]

    wide_ref[:rows] = product(0)
    wide_ref[rows:] = product(1)
    factors = head_factors(wide_ref[...], gather_ref[...])
    for b, own in enumerate(per_branch(product(2))):
        v_ref[b] = own.astype(BF16)
    wide_ref[...] *= jnp.dot(factors, spread_ref[...], preferred_element_type=F32)
    for b, own in enumerate(per_branch(wide_ref[:rows])):
        own = own.reshape(-1, outs, share, width)
        for r in range(outs):
            mine = own[:, r].reshape(-1, width)
            for i, columns, masks in pair_masks():
                part = mine[:, i * LANES : (i + 2) * LANES]
                for side, mask in enumerate(masks):
                    gain = mask * q_gain_ref[:, columns]
                    q_ref[r, b, i, side] = (part * gain).astype(BF16)
    for b, own in enumerate(per_branch(wide_ref[rows:])):
        k_ref[b] = (own * k_gain_ref[...]).astype(BF16)


def head_shapes(xs, outs):
    _, branch, share, width = xs[0].shape
    tokens = sum(x.shape[0] for x in xs) * share
    queries = (outs, branch, HEADS // 2, 2, tokens // outs, 2 * LANES)
    return [VMEM(shape, BF16) for shape in (queries, *[(branch, tokens, width)] * 2)]


def wide_shape(xs):
    _, branch, share, width = xs[0].shape
    return VMEM((2 * sum(x.shape[0] for x in xs) * branch * share, width), F32)


def heads_kernel(ins, outs, *refs):
    heads(refs[:ins], outs, *refs[ins:])


def make_heads(xs, tables, outs):
    return pl.pallas_call(
        functools.partial(heads_kernel, len(xs), outs),
        out_shape=head_shapes(xs, outs),
        in_specs=[pl.BlockSpec(memory_space=VMEM)] * (len(xs) + len(tables)),
        out_specs=[pl.BlockSpec(memory_space=VMEM)] * 3,
        scratch_shapes=[wide_shape(xs)],
        compiler_params=params(10),
        name="heads",
    )(*xs, *tables)


def attend_kernel(r, places, share, lead, *refs):
    *in_refs, scores_ref, probs_ref = refs
    lead_ref = None if lead is None else in_refs.pop()
    out_ref = in_refs.pop()
    groups = [in_refs[at : at + 3] for at in range(0, len(in_refs), 3)]
    _, branch, tokens, queries = scores_ref.shape[0], *out_ref.shape[1:2], *scores_ref.shape[1:]
    frames = tokens // share
    width = out_ref.shape[-1]
    same = lax.broadcasted_iota(jnp.int32, (share, queries), 0) == lax.rem(
        lax.broadcasted_iota(jnp.int32, (share, queries), 1), share
    )

    def rows_of(which, b, columns):
        return jnp.concatenate([group[which][b, :, columns] for group in groups], axis=0)

    def queries_of(b, i):
        return jnp.concatenate(
            [group[0][r, b, i, side] for side in range(2) for group in groups], axis=0
        )

    def emit(b, at, block):
        block = block.astype(BF16).reshape(-1, share, LANES)
        if places is None:
            out_ref[:, b, :, pl.ds(at, LANES)] = block
            return
        for slot, place in enumerate(places):
            out_ref[place, b, :, pl.ds(at, LANES)] = block[slot]
            if place == lead:
                lead_ref[0, b, :, pl.ds(at, LANES)] = block[slot]

    steps = [(i, columns, masks, b) for i, columns, masks in pair_masks() for b in range(branch)]
    carry = [None] * branch

    def score(at):
        i, columns, _, b = steps[at]
        scores_ref[at] = lax.dot_general(
            rows_of(1, b, columns),
            queries_of(b, i),
            (((1,), (1,)), ((), ())),
            preferred_element_type=F32,
        )

    def weigh(at):
        scores = scores_ref[at].reshape(frames, share, queries)
        top = jnp.max(scores, axis=0)
        weights = jnp.exp2((scores - top) * (HEAD_DIM ** (-0.5) * LOG2_E))
        total = jnp.sum(weights, axis=0)
        probs = weights * jnp.where(same, 1.0 / total, 0.0)
        probs_ref[at] = probs.reshape(tokens, queries).astype(BF16)

    def mix(at):
        i, columns, masks, b = steps[at]
        mixed = lax.dot_general(
            probs_ref[at],
            rows_of(2, b, columns),
            (((0,), (0,)), ((), ())),
            preferred_element_type=F32,
        )
        half = queries // 2
        mixed = jnp.where(
            masks[0] > 0.0, mixed[:half], jnp.where(masks[1] > 0.0, mixed[half:], 0.0)
        )
        block = mixed[:, :LANES]
        if carry[b] is not None:
            block = block + carry[b]
        carry[b] = mixed[:, LANES:]
        emit(b, i * LANES, block)

    for at in range(len(steps) + 2):
        if at < len(steps):
            score(at)
        if 0 <= at - 1 < len(steps):
            weigh(at - 1)
        if 0 <= at - 2:
            mix(at - 2)
    for b in range(branch):
        emit(b, width - LANES, carry[b])


def attend(r, groups, places, frames, share, outs, lead=None):
    branch, _, width = groups[0][1].shape
    tokens = frames * share
    steps, queries = branch * HEADS // 2, 2 * tokens // outs
    flat = [array for group in groups for array in group]
    shapes = [VMEM((frames // outs, branch, share, width), BF16)]
    if lead is not None:
        shapes.append(VMEM((1, branch, share, width), BF16))
    return pl.pallas_call(
        functools.partial(attend_kernel, r, places, share, lead),
        out_shape=shapes,
        in_specs=[pl.BlockSpec(memory_space=VMEM)] * len(flat),
        out_specs=[pl.BlockSpec(memory_space=VMEM)] * len(shapes),
        scratch_shapes=[
            VMEM((steps, tokens, queries), F32),
            VMEM((steps, tokens, queries), BF16),
        ],
        compiler_params=params(10),
        name="attend",
    )(*flat)


def project_kernel(ins, *refs):
    x_refs, (w_ref, gate_ref, residual_ref, out_ref) = refs[:ins], refs[ins:]
    _, branch, share, _ = x_refs[0].shape
    output = jnp.dot(gather_rows(x_refs), w_ref[...], preferred_element_type=F32)
    gated = (gate_ref[...] * output).reshape(-1, branch, share, output.shape[-1])
    for b in range(branch):
        out_ref[b] = residual_ref[b] + gated[:, b].reshape(out_ref.shape[1:])


def project(xs, w_proj, gate_row, rows):
    branch, patches, width = rows.shape
    cols = 384
    return pl.pallas_call(
        functools.partial(project_kernel, len(xs)),
        out_shape=jax.ShapeDtypeStruct(rows.shape, F32),
        grid=(width // cols,),
        in_specs=[pl.BlockSpec(x.shape, lambda j: (0, 0, 0, 0)) for x in xs]
        + [
            pl.BlockSpec((width, cols), lambda j: (0, j)),
            pl.BlockSpec((1, cols), lambda j: (0, j)),
            pl.BlockSpec((branch, patches, cols), lambda j: (0, 0, j)),
        ],
        out_specs=pl.BlockSpec((branch, patches, cols), lambda j: (0, 0, j)),
        compiler_params=params(12),
        name="project",
    )(*xs, w_proj, gate_row, rows)


def project_part_kernel(places, ins, *refs):
    x_refs, (w_ref, gate_ref, residual_ref) = refs[:ins], refs[ins : ins + 3]
    out_hbm, buffer_ref, sems = refs[-3:]
    _, branch, share, width = x_refs[0].shape
    x = gather_rows(x_refs)
    core = lax.rem(lax.axis_index("seq"), 2)
    cols = width // 3
    copies = []
    for at in range(0, width, cols):
        columns = pl.ds(at, cols)
        output = jnp.dot(x, w_ref[:, columns], preferred_element_type=F32)
        gated = (gate_ref[:, columns] * output).reshape(-1, 2, branch, share, cols)
        for slot, j in enumerate(places):
            start = pl.multiple_of((block_of(j, 0, True) - core) * share, 2 * share)
            for b in range(branch):
                for r in range(2):
                    own = pl.multiple_of(jnp.bitwise_xor(core, r) * share, share)
                    block = pl.ds(pl.multiple_of(start + own, share), share)
                    buffer_ref[slot, b, pl.ds(own, share), columns] = (
                        residual_ref[b, block, columns] + gated[slot, r, b]
                    )
                copies.append(
                    pltpu.make_async_copy(
                        buffer_ref.at[slot, b, :, columns],
                        out_hbm.at[b, pl.ds(start, 2 * share), columns],
                        sems.at[len(copies)],
                    )
                )
                copies[-1].start()
    for copy in copies:
        copy.wait()


def project_part(xs, places, w_proj, gate_row, rows, before):
    branch, _, width = rows.shape
    share = xs[0].shape[2]
    hbm = pl.BlockSpec(memory_space=pltpu.HBM)
    return pl.pallas_call(
        functools.partial(project_part_kernel, places, len(xs)),
        out_shape=pltpu.HBM(rows.shape, F32),
        in_specs=[pl.BlockSpec(memory_space=VMEM)] * (len(xs) + 3) + [hbm] * len(before),
        out_specs=hbm,
        scratch_shapes=[
            VMEM((len(places), branch, 2 * share, width), F32),
            pltpu.SemaphoreType.DMA((3 * branch * len(places),)),
        ],
        input_output_aliases={len(xs) + 3: 0} if before else {},
        compiler_params=params(6),
        name="project",
    )(*xs, w_proj, gate_row, rows, *before)


def body(n, exchange, residual, w_qkv, w_proj, q_gain, k_gain, step_mods, timestep):
    rows = residual[:, 0]
    share = rows.shape[1] // n
    if not exchange:
        swap = functools.partial(
            lax.all_to_all, axis_name="seq", split_axis=0, concat_axis=0, tiled=True
        )
        parts, *_, gate_row, _ = modulate(rows, step_mods, timestep, n, exchange)
        tables = w_qkv, *make_tables(q_gain, k_gain, gate_row)
        group = make_heads([swap(parts)], tables, 1)
        attended = swap(attend(0, [group], None, n, share, 1)[0])
        return project([attended], w_proj, gate_row, rows)[:, None]

    places = (0, *send_order(n))
    first, last = places[: n // 4], places[n // 4 :]
    lead = places[1]
    give, scale_row, shift_row, gate_row, held = modulate(rows, step_mods, timestep, n, exchange)
    parts = swap_parts(
        n, give, lambda: modulate_kept(held, scale_row, shift_row, give, lead)
    )
    tables = w_qkv, *make_tables(q_gain, k_gain, gate_row)
    early = make_heads([part for j in first for part in parts[j]], tables, 2)
    groups = early, make_heads([part for j in last for part in parts[j]], tables, 2)
    (give,) = attend(1, groups, places, n, share, 2)
    parts = swap_parts(n, give, lambda: attend(0, groups, places, n, share, 2, lead))
    out = []
    for chips in (first, last):
        own = [part for j in chips for part in parts[j]]
        out = [project_part(own, chips, w_proj, gate_row, rows, out)]
    return out[0][:, None]


def solution(mesh):
    in_specs = (P("groups", "seq", None, None), P(), P(), P(), P(), P(), P("groups"))
    out_specs = P("groups", "seq", None, None)
    n = mesh.shape["seq"]

    def step(residual, *others):
        share = residual.shape[2] // n
        exchange = 8 <= n <= 32 and n & (n - 1) == 0 and share % 8 == 0
        run = jax.shard_map(
            functools.partial(body, n, exchange),
            mesh=mesh,
            in_specs=in_specs,
            out_specs=out_specs,
            check_vma=False,
        )
        return run(residual, *others)

    return step
```

```python
import functools

import jax
import jax.numpy as jnp
from jax import lax
from jax.experimental import pallas as pl
from jax.experimental.pallas import tpu as pltpu
from jax.sharding import PartitionSpec as P

HEADS = 16
HEAD_DIM = 72
LANES = 128
LOG2_E = 1.4426950408889634
F32 = jnp.float32
BF16 = jnp.bfloat16
VMEM = pltpu.VMEM


def params(mebibytes):
    return pltpu.CompilerParams(vmem_limit_bytes=mebibytes << 20)


def in_hbm(array):
    return pltpu.with_memory_space_constraint(array, pltpu.HBM)


def block_of(j, r, exchange):
    if not exchange:
        return j
    me = lax.axis_index("seq")
    return jnp.bitwise_xor(me, 2 * j + r)


def modulate_rows(rows_ref, scale_row, shift_row, out_ref, r, exchange, branches):
    count, _, share, width = out_ref.shape
    group = 1 if exchange else max(1, 32 // share)
    for b in branches:
        for j in range(0, count, group):
            start = block_of(j, r, exchange) * share
            if exchange:
                start = pl.multiple_of(start, share)
            rows = rows_ref[b, pl.ds(start, group * share)]
            centre = jnp.mean(rows, axis=-1, keepdims=True)
            centred = rows - centre
            variance = jnp.mean(centred * centred, axis=-1, keepdims=True)
            normed = centred * lax.rsqrt(variance + 1e-06) * scale_row + shift_row
            out_ref[j : j + group, b] = normed.reshape(group, share, width).astype(BF16)


def modulate_kernel(exchange, step_ref, rows_hbm, mods_hbm, out_ref, *refs):
    scale_ref, shift_ref, gate_ref, rows_ref, mods_ref, sems = refs
    branch = rows_ref.shape[0]

    def fetch(b):
        return pltpu.make_async_copy(rows_hbm.at[b], rows_ref.at[b], sems.at[b])

    steps, tile = mods_hbm.shape[1], mods_ref.shape[1]
    whole = steps // tile * tile
    step = step_ref[0]

    def fetch_mods(act):
        def full():
            block = pl.ds(pl.multiple_of(step // tile * tile, tile), tile)
            act(pltpu.make_async_copy(mods_hbm.at[:, block], mods_ref, sems.at[branch]))

        def short():
            block = pl.ds(whole, steps - whole)
            part = mods_ref.at[:, pl.ds(0, steps - whole)]
            act(pltpu.make_async_copy(mods_hbm.at[:, block], part, sems.at[branch]))

        pl.when(step < whole)(full)
        if whole < steps:
            pl.when(step >= whole)(short)

    fetch_mods(lambda copy: copy.start())
    fetch(0).start()
    for b in range(1, branch):
        fetch(b).start()
    fetch_mods(lambda copy: copy.wait())
    step = pl.ds(lax.rem(step, tile), 1)
    shift_row, scale_row = mods_ref[0, step, :], 1.0 + mods_ref[1, step, :]
    shift_ref[...] = shift_row
    scale_ref[...] = scale_row
    gate_ref[...] = mods_ref[2, step, :]
    for b in range(branch):
        fetch(b).wait()
        modulate_rows(rows_ref, scale_row, shift_row, out_ref, 1, exchange, [b])


def modulate(rows, step_mods, timestep, n, exchange):
    branch, patches, width = rows.shape
    outs = 2 if exchange else 1
    row = VMEM((1, width), F32)
    return pl.pallas_call(
        functools.partial(modulate_kernel, exchange),
        out_shape=[
            VMEM((n // outs, branch, patches // n, width), BF16),
            row,
            row,
            row,
            VMEM((branch, patches, width), F32),
        ],
        in_specs=[pl.BlockSpec(memory_space=pltpu.SMEM)]
        + [pl.BlockSpec(memory_space=pltpu.HBM)] * 2,
        out_specs=[pl.BlockSpec(memory_space=VMEM)] * 5,
        scratch_shapes=[
            VMEM((3, 8, width), F32),
            pltpu.SemaphoreType.DMA((branch + 1,)),
        ],
        compiler_params=params(8),
        name="modulate",
    )(timestep, in_hbm(rows), in_hbm(jnp.swapaxes(step_mods, 0, 1)))


def keep_kernel(lead, rows_ref, scale_ref, shift_ref, out_ref, lead_ref):
    branches = range(rows_ref.shape[0])
    modulate_rows(rows_ref, scale_ref[...], shift_ref[...], out_ref, 0, True, branches)
    lead_ref[0] = out_ref[lead]


def modulate_kept(rows, scale_row, shift_row, like, lead):
    return pl.pallas_call(
        functools.partial(keep_kernel, lead),
        out_shape=[VMEM(like.shape, BF16), VMEM((1, *like.shape[1:]), BF16)],
        in_specs=[pl.BlockSpec(memory_space=VMEM)] * 3,
        out_specs=[pl.BlockSpec(memory_space=VMEM)] * 2,
        compiler_params=params(4),
        name="keep",
    )(rows, scale_row, shift_row)


def tables_kernel(after_ref, q_gain_hbm, k_gain_hbm, *refs):
    gather_ref, spread_ref, q_row_ref, k_row_ref, line_ref, sems = refs
    del after_ref
    gains = [
        pltpu.make_async_copy(gain, line_ref.at[at], sems.at[at])
        for at, gain in enumerate((q_gain_hbm, k_gain_hbm))
    ]
    for copy in gains:
        copy.start()
    gather_ref[...] = head_of(gather_ref.shape, 0)
    spread_ref[...] = head_of(spread_ref.shape, 1)
    for at, row_ref in enumerate((q_row_ref, k_row_ref)):
        gains[at].wait()
        row_ref[...] = line_ref[at].reshape(row_ref.shape)


def make_tables(q_gain, k_gain, after):
    width = q_gain.shape[0]
    hbm = pl.BlockSpec(memory_space=pltpu.HBM)
    return pl.pallas_call(
        tables_kernel,
        out_shape=[
            VMEM((width, LANES), BF16),
            VMEM((LANES, width), BF16),
            VMEM((1, width), F32),
            VMEM((1, width), F32),
        ],
        in_specs=[pl.BlockSpec(memory_space=VMEM), hbm, hbm],
        out_specs=[pl.BlockSpec(memory_space=VMEM)] * 4,
        scratch_shapes=[VMEM((2, width), F32), pltpu.SemaphoreType.DMA((2,))],
        compiler_params=params(2),
        name="tables",
    )(after, in_hbm(q_gain), in_hbm(k_gain))


def pack_kernel(lead, keep_ref, got_ref, *out_refs):
    for j, out_ref in enumerate(out_refs):
        if j == lead:
            out_ref[0] = got_ref[j]
        else:
            out_ref[0] = keep_ref[j]
            out_ref[1] = got_ref[j]


def pack(keep, got, lead):
    count, *part = keep.shape
    return pl.pallas_call(
        functools.partial(pack_kernel, lead),
        out_shape=[VMEM((1 if j == lead else 2, *part), keep.dtype) for j in range(count)],
        in_specs=[pl.BlockSpec(memory_space=VMEM)] * 2,
        out_specs=[pl.BlockSpec(memory_space=VMEM)] * count,
        compiler_params=params(1),
        cost_estimate=pl.CostEstimate(flops=10**10, bytes_accessed=10**7, transcendentals=0),
        name="pack",
    )(keep, got)


def send_order(n):
    far, near = [*range(n // 4, n // 2)], [*range(1, n // 4)]
    return [*far[:2], *near[-1:], *far[:1:-1], *near[-2::-1]]


def swap_parts(n, give, make_keep):
    def send(j, part):
        return lax.ppermute(part, "seq", [(s, s ^ (2 * j)) for s in range(n)])

    order = send_order(n)
    got = lax.ppermute(give, "seq", [(s, s ^ 1) for s in range(n)])
    keep, first = make_keep()
    first = send(order[0], first)
    parts = [[part] for part in pack(keep, got, order[0])]
    for j in order:
        parts[j] = [send(j, parts[j][0])]
    parts[order[0]].insert(0, first)
    return parts


def gather_rows(x_refs):
    return jnp.concatenate([ref[...].reshape(-1, ref.shape[-1]) for ref in x_refs], axis=0)


def head_of(shape, feature_dim):
    feature = lax.broadcasted_iota(jnp.int32, shape, feature_dim)
    place = lax.broadcasted_iota(jnp.int32, shape, 1 - feature_dim)
    first = lax.rem(place, HEADS) * HEAD_DIM
    inside = (feature >= first) & (feature < first + HEAD_DIM) & (place < 2 * HEADS)
    return jnp.where(inside, 1.0, 0.0).astype(BF16)


def high_low(wide):
    high = wide.astype(BF16)
    return high, wide - high.astype(F32)


def head_factors(vectors, gather):
    high, low = high_low(vectors * vectors)
    rows = vectors.shape[0]
    stacked = jnp.concatenate([high, low.astype(BF16)], axis=0)
    square = jnp.dot(stacked, gather, preferred_element_type=F32)
    square = square[:rows] + square[rows:]
    high, low = high_low(lax.rsqrt(square * (1.0 / HEAD_DIM) + 1e-06))
    place = lax.broadcasted_iota(jnp.int32, low.shape, 1)
    return jnp.where(place < HEADS, high.astype(F32), low).astype(BF16)


def pair_masks():
    lane = lax.broadcasted_iota(jnp.int32, (1, 2 * LANES), 1)
    for i in range(HEADS // 2):
        masks = []
        for h in (2 * i, 2 * i + 1):
            start = h * HEAD_DIM - i * LANES
            masks.append(jnp.where((lane >= start) & (lane < start + HEAD_DIM), 1.0, 0.0))
        yield i, pl.ds(i * LANES, 2 * LANES), masks


def heads(x_refs, outs, *refs):
    w_ref, gather_ref, spread_ref, q_gain_ref, k_gain_ref, q_ref, k_ref, v_ref, wide_ref = refs
    _, branch, share, width = x_refs[0].shape
    x = gather_rows(x_refs)
    rows = x.shape[0]

    def product(part):
        columns = w_ref[:, part * width : (part + 1) * width]
        return jnp.dot(x, columns, preferred_element_type=F32)

    def per_branch(values):
        values = values.reshape(-1, branch, share, width)
        return [values[:, b].reshape(-1, width) for b in range(branch)]

    wide_ref[:rows] = product(0)
    wide_ref[rows:] = product(1)
    factors = head_factors(wide_ref[...], gather_ref[...])
    for b, own in enumerate(per_branch(product(2))):
        v_ref[b] = own.astype(BF16)
    wide_ref[...] *= jnp.dot(factors, spread_ref[...], preferred_element_type=F32)
    for b, own in enumerate(per_branch(wide_ref[:rows])):
        own = own.reshape(-1, outs, share, width)
        for r in range(outs):
            mine = own[:, r].reshape(-1, width)
            for i, columns, masks in pair_masks():
                part = mine[:, i * LANES : (i + 2) * LANES]
                for side, mask in enumerate(masks):
                    gain = mask * q_gain_ref[:, columns]
                    q_ref[r, b, i, side] = (part * gain).astype(BF16)
    for b, own in enumerate(per_branch(wide_ref[rows:])):
        k_ref[b] = (own * k_gain_ref[...]).astype(BF16)


def head_shapes(xs, outs):
    _, branch, share, width = xs[0].shape
    tokens = sum(x.shape[0] for x in xs) * share
    queries = (outs, branch, HEADS // 2, 2, tokens // outs, 2 * LANES)
    return [VMEM(shape, BF16) for shape in (queries, *[(branch, tokens, width)] * 2)]


def wide_shape(xs):
    _, branch, share, width = xs[0].shape
    return VMEM((2 * sum(x.shape[0] for x in xs) * branch * share, width), F32)


def heads_kernel(ins, outs, *refs):
    heads(refs[:ins], outs, *refs[ins:])


def make_heads(xs, tables, outs):
    return pl.pallas_call(
        functools.partial(heads_kernel, len(xs), outs),
        out_shape=head_shapes(xs, outs),
        in_specs=[pl.BlockSpec(memory_space=VMEM)] * (len(xs) + len(tables)),
        out_specs=[pl.BlockSpec(memory_space=VMEM)] * 3,
        scratch_shapes=[wide_shape(xs)],
        compiler_params=params(10),
        name="heads",
    )(*xs, *tables)


def attend_kernel(r, places, share, lead, *refs):
    *in_refs, scores_ref, probs_ref = refs
    lead_ref = None if lead is None else in_refs.pop()
    out_ref = in_refs.pop()
    groups = [in_refs[at : at + 3] for at in range(0, len(in_refs), 3)]
    _, branch, tokens, queries = scores_ref.shape[0], *out_ref.shape[1:2], *scores_ref.shape[1:]
    frames = tokens // share
    width = out_ref.shape[-1]
    same = lax.broadcasted_iota(jnp.int32, (share, queries), 0) == lax.rem(
        lax.broadcasted_iota(jnp.int32, (share, queries), 1), share
    )

    def rows_of(which, b, columns):
        return jnp.concatenate([group[which][b, :, columns] for group in groups], axis=0)

    def queries_of(b, i):
        return jnp.concatenate(
            [group[0][r, b, i, side] for side in range(2) for group in groups], axis=0
        )

    def emit(b, at, block):
        block = block.astype(BF16).reshape(-1, share, LANES)
        if places is None:
            out_ref[:, b, :, pl.ds(at, LANES)] = block
            return
        for slot, place in enumerate(places):
            out_ref[place, b, :, pl.ds(at, LANES)] = block[slot]
            if place == lead:
                lead_ref[0, b, :, pl.ds(at, LANES)] = block[slot]

    steps = [(i, columns, masks, b) for i, columns, masks in pair_masks() for b in range(branch)]
    carry = [None] * branch

    def score(at):
        i, columns, _, b = steps[at]
        scores_ref[at] = lax.dot_general(
            rows_of(1, b, columns),
            queries_of(b, i),
            (((1,), (1,)), ((), ())),
            preferred_element_type=F32,
        )

    def weigh(at):
        scores = scores_ref[at].reshape(frames, share, queries)
        top = jnp.max(scores, axis=0)
        weights = jnp.exp2((scores - top) * (HEAD_DIM ** (-0.5) * LOG2_E))
        total = jnp.sum(weights, axis=0)
        probs = weights * jnp.where(same, 1.0 / total, 0.0)
        probs_ref[at] = probs.reshape(tokens, queries).astype(BF16)

    def mix(at):
        i, columns, masks, b = steps[at]
        mixed = lax.dot_general(
            probs_ref[at],
            rows_of(2, b, columns),
            (((0,), (0,)), ((), ())),
            preferred_element_type=F32,
        )
        half = queries // 2
        mixed = jnp.where(
            masks[0] > 0.0, mixed[:half], jnp.where(masks[1] > 0.0, mixed[half:], 0.0)
        )
        block = mixed[:, :LANES]
        if carry[b] is not None:
            block = block + carry[b]
        carry[b] = mixed[:, LANES:]
        emit(b, i * LANES, block)

    for at in range(len(steps) + 2):
        if at < len(steps):
            score(at)
        if 0 <= at - 1 < len(steps):
            weigh(at - 1)
        if 0 <= at - 2:
            mix(at - 2)
    for b in range(branch):
        emit(b, width - LANES, carry[b])


def attend(r, groups, places, frames, share, outs, lead=None):
    branch, _, width = groups[0][1].shape
    tokens = frames * share
    steps, queries = branch * HEADS // 2, 2 * tokens // outs
    flat = [array for group in groups for array in group]
    shapes = [VMEM((frames // outs, branch, share, width), BF16)]
    if lead is not None:
        shapes.append(VMEM((1, branch, share, width), BF16))
    return pl.pallas_call(
        functools.partial(attend_kernel, r, places, share, lead),
        out_shape=shapes,
        in_specs=[pl.BlockSpec(memory_space=VMEM)] * len(flat),
        out_specs=[pl.BlockSpec(memory_space=VMEM)] * len(shapes),
        scratch_shapes=[
            VMEM((steps, tokens, queries), F32),
            VMEM((steps, tokens, queries), BF16),
        ],
        compiler_params=params(10),
        name="attend",
    )(*flat)


def project_kernel(ins, *refs):
    x_refs, (w_ref, gate_ref, residual_ref, out_ref) = refs[:ins], refs[ins:]
    _, branch, share, _ = x_refs[0].shape
    output = jnp.dot(gather_rows(x_refs), w_ref[...], preferred_element_type=F32)
    gated = (gate_ref[...] * output).reshape(-1, branch, share, output.shape[-1])
    for b in range(branch):
        out_ref[b] = residual_ref[b] + gated[:, b].reshape(out_ref.shape[1:])


def project(xs, w_proj, gate_row, rows):
    branch, patches, width = rows.shape
    cols = 384
    return pl.pallas_call(
        functools.partial(project_kernel, len(xs)),
        out_shape=jax.ShapeDtypeStruct(rows.shape, F32),
        grid=(width // cols,),
        in_specs=[pl.BlockSpec(x.shape, lambda j: (0, 0, 0, 0)) for x in xs]
        + [
            pl.BlockSpec((width, cols), lambda j: (0, j)),
            pl.BlockSpec((1, cols), lambda j: (0, j)),
            pl.BlockSpec((branch, patches, cols), lambda j: (0, 0, j)),
        ],
        out_specs=pl.BlockSpec((branch, patches, cols), lambda j: (0, 0, j)),
        compiler_params=params(12),
        name="project",
    )(*xs, w_proj, gate_row, rows)


def project_part_kernel(places, ins, *refs):
    x_refs, (w_ref, gate_ref, residual_ref) = refs[:ins], refs[ins : ins + 3]
    out_hbm, buffer_ref, sems = refs[-3:]
    _, branch, share, width = x_refs[0].shape
    x = gather_rows(x_refs)
    core = lax.rem(lax.axis_index("seq"), 2)
    cols = width // 3
    copies = []
    for at in range(0, width, cols):
        columns = pl.ds(at, cols)
        output = jnp.dot(x, w_ref[:, columns], preferred_element_type=F32)
        gated = (gate_ref[:, columns] * output).reshape(-1, 2, branch, share, cols)
        for slot, j in enumerate(places):
            start = pl.multiple_of((block_of(j, 0, True) - core) * share, 2 * share)
            for b in range(branch):
                for r in range(2):
                    own = pl.multiple_of(jnp.bitwise_xor(core, r) * share, share)
                    block = pl.ds(pl.multiple_of(start + own, share), share)
                    buffer_ref[slot, b, pl.ds(own, share), columns] = (
                        residual_ref[b, block, columns] + gated[slot, r, b]
                    )
                copies.append(
                    pltpu.make_async_copy(
                        buffer_ref.at[slot, b, :, columns],
                        out_hbm.at[b, pl.ds(start, 2 * share), columns],
                        sems.at[len(copies)],
                    )
                )
                copies[-1].start()
    for copy in copies:
        copy.wait()


def project_part(xs, places, w_proj, gate_row, rows, before):
    branch, _, width = rows.shape
    share = xs[0].shape[2]
    hbm = pl.BlockSpec(memory_space=pltpu.HBM)
    return pl.pallas_call(
        functools.partial(project_part_kernel, places, len(xs)),
        out_shape=pltpu.HBM(rows.shape, F32),
        in_specs=[pl.BlockSpec(memory_space=VMEM)] * (len(xs) + 3) + [hbm] * len(before),
        out_specs=hbm,
        scratch_shapes=[
            VMEM((len(places), branch, 2 * share, width), F32),
            pltpu.SemaphoreType.DMA((3 * branch * len(places),)),
        ],
        input_output_aliases={len(xs) + 3: 0} if before else {},
        compiler_params=params(6),
        name="project",
    )(*xs, w_proj, gate_row, rows, *before)


def body(n, exchange, residual, w_qkv, w_proj, q_gain, k_gain, step_mods, timestep):
    rows = residual[:, 0]
    share = rows.shape[1] // n
    if not exchange:
        swap = functools.partial(
            lax.all_to_all, axis_name="seq", split_axis=0, concat_axis=0, tiled=True
        )
        parts, *_, gate_row, _ = modulate(rows, step_mods, timestep, n, exchange)
        tables = w_qkv, *make_tables(q_gain, k_gain, gate_row)
        group = make_heads([swap(parts)], tables, 1)
        attended = swap(attend(0, [group], None, n, share, 1)[0])
        return project([attended], w_proj, gate_row, rows)[:, None]

    places = (0, *send_order(n))
    first, last = places[: n // 4], places[n // 4 :]
    lead = places[1]
    give, scale_row, shift_row, gate_row, held = modulate(rows, step_mods, timestep, n, exchange)
    parts = swap_parts(
        n, give, lambda: modulate_kept(held, scale_row, shift_row, give, lead)
    )
    tables = w_qkv, *make_tables(q_gain, k_gain, gate_row)
    early = make_heads([part for j in first for part in parts[j]], tables, 2)
    groups = early, make_heads([part for j in last for part in parts[j]], tables, 2)
    (give,) = attend(1, groups, places, n, share, 2)
    parts = swap_parts(n, give, lambda: attend(0, groups, places, n, share, 2, lead))
    out = []
    for chips in (first, last):
        own = [part for j in chips for part in parts[j]]
        out = [project_part(own, chips, w_proj, gate_row, rows, out)]
    return out[0][:, None]


def solution(mesh):
    in_specs = (P("groups", "seq", None, None), P(), P(), P(), P(), P(), P("groups"))
    out_specs = P("groups", "seq", None, None)
    n = mesh.shape["seq"]

    def step(residual, *others):
        share = residual.shape[2] // n
        exchange = 8 <= n <= 32 and n & (n - 1) == 0 and share % 8 == 0
        run = jax.shard_map(
            functools.partial(body, n, exchange),
            mesh=mesh,
            in_specs=in_specs,
            out_specs=out_specs,
            check_vma=False,
        )
        return run(residual, *others)

    return step
```
